128 devices in a mesh: goal: 8 (over z, core), cand: 16 (over x, y).
Axes of the slice: x: 4, y: 4, z: 4, core: 2. Of those that a mesh axis runs over, the one named last changes fastest.
Arguments:
- dec_states: bfloat16 [8, 32, 24, 4096], P('goal', 'cand'), may hold values from -18 to 18
- memory: bfloat16 [8, 512, 4096], P('goal', 'cand'), may hold values from -18 to 18
- counts: int32 [8], P('goal'), may hold values from 2 to 30, as said below
- rank: int32 [8, 32], P('goal'), may hold values from 0 to 31, each once within a row
- visits: int32 [8, 32], P('goal'), may hold values from 1 to 64
- w_query: bfloat16 [4096, 4096], P(None, 'cand'), may hold values from -1 to 1
- w_key: bfloat16 [4096, 4096], P(None, 'cand'), may hold values from -1 to 1
- w_value: bfloat16 [4096, 4096], P(None, 'cand'), may hold values from -0.3125 to 0.3125
- w_out: bfloat16 [4096, 4096], P('cand'), may hold values from -0.25 to 0.25
- gain: float32 [4096], replicated, may hold values from 0.5 to 1.5
- w_score: float32 [4096], replicated, may hold values from -0.5 to 0.5
Outputs:
- log_probs: float32 [8, 32], P('goal', 'cand')
- goal_loss: float32 [8], P('goal')
- grad_query: bfloat16 [4096, 4096], P('goal', 'cand')
- grad_key: bfloat16 [4096, 4096], P('goal', 'cand')
- grad_value: bfloat16 [4096, 4096], P('goal', 'cand')
- grad_out: bfloat16 [4096, 4096], P('cand', 'goal')
The draws below stay inside these ranges and needn't reach their ends.
Inputs may be any that keep to these rules, and one draw needn't show every extreme that they name: `counts`: every goal has 2 to 30 candidates, and some goal has exactly 30. `rank`: each goal's row is a permutation; the slot holding candidate number j is live when j is below the goal's count.
All inputs are finite; a program needn't handle non-finite values.
Results may differ from the reference program's by a relative error of at most 0.015.
Values may be sent and summed in bfloat16 or wider, within the bound.
No kernel may reach another device: no remote copies, remote signals or barrier semaphores. Data moves between devices by JAX's collectives and lax.ppermute only.
A program may use at most 128 MiB of HBM per device.

```python
import jax
import jax.numpy as jnp
from jax import lax

D = 4096
HEADS = 64
HD = 64
MEM = 512
SLOTS = 32
TACT = 24
GOALS = 8
HEADS_DEV = 4
N_CAND = 16


def score_base(key):
    return jnp.clip(jax.random.normal(jax.random.fold_in(key, 41), (D,), jnp.float32), -4.0, 4.0)


def draw_dec_states(key, part):
    values = jnp.clip(jax.random.normal(jax.random.fold_in(key, 1), (GOALS, SLOTS, TACT, D), jnp.float32), -4.0, 4.0)
    slope = jax.random.uniform(jax.random.fold_in(key, 43), (GOALS, SLOTS), jnp.float32, -2.0, 2.0)
    values = values + slope[:, :, None, None] * score_base(key)[None, None, None, :]
    return values.astype(jnp.bfloat16)


def draw_memory(key, part):
    values = jnp.clip(jax.random.normal(jax.random.fold_in(key, 2), (GOALS, MEM, D), jnp.float32), -4.0, 4.0)
    return values.astype(jnp.bfloat16)


def query_base(key):
    return jnp.clip(jax.random.normal(jax.random.fold_in(key, 21), (D, D), jnp.float32), -4.0, 4.0)


def draw_w_query(key, part):
    return (query_base(key) / jnp.sqrt(1.0 * D)).astype(jnp.bfloat16)


def draw_w_key(key, part):
    fresh = jnp.clip(jax.random.normal(jax.random.fold_in(key, 22), (D, D), jnp.float32), -4.0, 4.0)
    return (fresh / jnp.sqrt(1.0 * D)).astype(jnp.bfloat16)


def draw_w_score(key, part):
    values = score_base(key)
    return 0.005 * values


def draw_counts(key, part):
    values = jax.random.randint(jax.random.fold_in(key, 51), (GOALS,), 2, 31)
    chosen = jax.random.randint(jax.random.fold_in(key, 52), (), 0, GOALS)
    return jnp.where(jnp.arange(GOALS) == chosen, 30, values).astype(jnp.int32)


def with_ends(result, stream_key, least, high):
    longest = result.shape.index(max(result.shape))
    spots = []
    for shift in (0, 1):
        where = [jax.random.randint(jax.random.fold_in(stream_key, axis), (), 0, length) for axis, length in enumerate(result.shape)]
        where[longest] = (where[longest] + shift) % result.shape[longest]
        spots.append(tuple(where))
    return result.at[spots[0]].set(least).at[spots[1]].set(high)


def block_scale(stream_key, extent, shards, smallest, high):
    loudness, own = 1.0, jax.random.fold_in(stream_key, 6)
    for dim, blocks in shards:
        heights = jnp.exp(jax.random.uniform(jax.random.fold_in(own, dim), (blocks,), jnp.float32, smallest / len(shards), high / len(shards)))
        loudness = loudness * jnp.repeat(heights, extent[dim] // blocks).reshape([-1 if axis == dim else 1 for axis in range(len(extent))])
    return loudness


def normal_values(rng, dims, deviation, limit, shards=(), held_as=jnp.bfloat16):
    array = jax.random.normal(rng, dims, jnp.float32) * deviation
    if len(shards) > 0:
        array = block_scale(rng, dims, shards, -0.22, 0.18) * array
    return jnp.clip(array, min=-limit, max=limit).astype(held_as)


def setup_inputs(seed: int = 0) -> dict:
    splits = jax.random.split(jax.random.key(seed), 12)
    return {
        "dec_states": draw_dec_states(jax.random.fold_in(splits[11], 71), 0),
        "memory": draw_memory(jax.random.fold_in(splits[11], 71), 0),
        "counts": draw_counts(jax.random.fold_in(splits[11], 71), 0),
        "rank": jax.vmap(lambda own: jax.random.permutation(own, SLOTS))(jax.random.split(splits[3], GOALS)).reshape((GOALS, SLOTS)).astype(jnp.int32),
        "visits": with_ends(jax.random.randint(splits[4], (GOALS, SLOTS), 1, 65), jax.random.fold_in(splits[4], 1), 1, 64).astype(jnp.int32),
        "w_query": draw_w_query(jax.random.fold_in(splits[11], 71), 0),
        "w_key": draw_w_key(jax.random.fold_in(splits[11], 71), 0),
        "w_value": normal_values(splits[7], (D, D), (D // 12) ** -0.5, 0.3125, ((1, 16),)),
        "w_out": normal_values(splits[8], (D, D), (D // 9) ** -0.5, 0.25, ((0, 16),)),
        "gain": jnp.clip(1.0 + 0.1 * jax.random.normal(splits[9], (D,), jnp.float32), 0.5, 1.5),
        "w_score": draw_w_score(jax.random.fold_in(splits[11], 71), 0),
    }


def token_terms(rows, attended, weighted):
    hidden = rows.astype(jnp.float32) + attended
    inverse = lax.rsqrt(lax.optimization_barrier(jnp.mean(hidden * hidden, axis=-1)) + 1e-06)
    raw = lax.optimization_barrier(jnp.sum(hidden * weighted[None, :], axis=-1))
    return (hidden, inverse, raw)

def goal_softmax(logits, live, visit):
    masked = jnp.where(live, logits, -1e+30)
    top_value = jnp.max(masked)
    exponent = jnp.where(live, jnp.exp(masked - top_value), 0.0)
    log_total = top_value + jnp.log(jnp.sum(exponent))
    log_weight = jnp.where(live, logits - log_total, 0.0)
    visit_mass = jnp.where(live, visit.astype(jnp.float32), 0.0)
    target = visit_mass / jnp.sum(visit_mass)
    loss = -jnp.sum(target * log_weight)
    logit_grad = jnp.where(live, jnp.exp(log_weight) - target, 0.0)
    return (log_weight, loss, logit_grad)

def norm_grad(hidden, inverse, raw, tok_grad, weighted, model_width):
    factor = inverse * inverse * inverse * tok_grad * raw / model_width
    return ((inverse * tok_grad)[:, None] * weighted[None, :] - hidden * factor[:, None]).astype(jnp.bfloat16)

def reference(dec_states, memory, counts, rank, visits, w_query, w_key, w_value, w_out, gain, w_score):
    weighted = gain.astype(jnp.float32) * w_score.astype(jnp.float32)
    scale = HD ** (-0.5)
    total_rows = SLOTS * TACT
    group = HEADS_DEV * HD

    def one_goal(totals, items):
        states, mem, count, order, visit = items
        rows = states.reshape(total_rows, D)
        query = jnp.dot(rows, w_query, preferred_element_type=jnp.float32).astype(jnp.bfloat16)
        key = jnp.dot(mem, w_key, preferred_element_type=jnp.float32).astype(jnp.bfloat16)
        value = jnp.dot(mem, w_value, preferred_element_type=jnp.float32).astype(jnp.bfloat16)
        query_heads = query.reshape(total_rows, HEADS, HD).astype(jnp.float32)
        key_heads = key.reshape(MEM, HEADS, HD).astype(jnp.float32)
        value_heads = value.reshape(MEM, HEADS, HD).astype(jnp.float32)
        scores = jnp.einsum('rhe,mhe->hrm', query_heads, key_heads) * scale
        softmaxed = jax.nn.softmax(scores, axis=-1)
        softmaxed_low = softmaxed.astype(jnp.bfloat16)
        mixed = jnp.einsum('hrm,mhe->rhe', softmaxed_low.astype(jnp.float32), value_heads)
        mixed = mixed.astype(jnp.bfloat16).reshape(total_rows, D)
        parts = jnp.einsum('rgc,gcd->grd', mixed.reshape(total_rows, N_CAND, group).astype(jnp.float32), w_out.reshape(N_CAND, group, D).astype(jnp.float32))
        attended = lax.optimization_barrier(jnp.sum(lax.optimization_barrier(parts.astype(jnp.bfloat16)).astype(jnp.float32), axis=0))
        hidden, inverse, raw = token_terms(rows, attended, weighted)
        logits = lax.optimization_barrier(jnp.mean((inverse * raw).reshape(SLOTS, TACT), axis=1))
        live = order < count
        log_weight, loss, logit_grad = goal_softmax(logits, live, visit)
        tok_grad = jnp.repeat(logit_grad / TACT, TACT, total_repeat_length=total_rows)
        hidden_grad = norm_grad(hidden, inverse, raw, tok_grad, weighted, D)
        mixed_grad = jnp.dot(hidden_grad, w_out.T, preferred_element_type=jnp.float32).astype(jnp.bfloat16)
        out_term = jnp.dot(mixed.T, hidden_grad, preferred_element_type=jnp.float32)
        grad_heads = mixed_grad.reshape(total_rows, HEADS, HD).astype(jnp.float32)
        prob_grad = jnp.einsum('rhe,mhe->hrm', grad_heads, value_heads)
        delta = lax.optimization_barrier(jnp.sum(softmaxed * prob_grad, axis=-1, keepdims=True))
        score_grad = (softmaxed * (prob_grad - delta) * scale).astype(jnp.bfloat16).astype(jnp.float32)
        query_grad = jnp.einsum('hrm,mhe->rhe', score_grad, key_heads).astype(jnp.bfloat16).reshape(total_rows, D)
        key_grad = jnp.einsum('hrm,rhe->mhe', score_grad, query_heads).astype(jnp.bfloat16).reshape(MEM, D)
        value_grad = jnp.einsum('hrm,rhe->mhe', softmaxed_low.astype(jnp.float32), grad_heads)
        value_grad = value_grad.astype(jnp.bfloat16).reshape(MEM, D)
        query_term = jnp.dot(rows.T, query_grad, preferred_element_type=jnp.float32)
        key_term = jnp.dot(mem.T, key_grad, preferred_element_type=jnp.float32)
        value_term = jnp.dot(mem.T, value_grad, preferred_element_type=jnp.float32)
        terms = (query_term, key_term, value_term, out_term)
        totals = tuple((total + lax.optimization_barrier(term.astype(jnp.bfloat16)).astype(jnp.float32) for total, term in zip(totals, terms)))
        return (totals, (log_weight, loss))
    zeros = tuple((jnp.zeros((D, D), jnp.float32) for index in range(4)))
    totals, outputs = lax.scan(one_goal, zeros, (dec_states, memory, counts, rank, visits))
    log_probs, goal_loss = outputs
    return (log_probs, goal_loss, totals[0].astype(jnp.bfloat16), totals[1].astype(jnp.bfloat16), totals[2].astype(jnp.bfloat16), totals[3].astype(jnp.bfloat16))
```

```python
import jax
import jax.numpy as jnp
from jax import lax
from jax.sharding import PartitionSpec as P

HD = 64


CAND_MASKS = (4, 12, 1, 3)
PART_ORDERS = ((0, 1, 2, 3), (1, 0, 3, 2), (2, 3, 0, 1), (3, 2, 1, 0))


def swap(values, axis, size, mask):
    return lax.ppermute(values, axis, [(i, i ^ mask) for i in range(size)])


def pair_bits(coordinate):
    high = coordinate >> 1
    return ((coordinate & 1) ^ high, high)


def slot_order():
    order = []
    for position in range(16):
        bits = [(position >> i) & 1 for i in range(4)]
        x = bits[0] ^ (3 * bits[1])
        y = bits[2] ^ (3 * bits[3])
        order.append(4 * x + y)
    return order


def gather_cand(own, bits):
    parts = [part[None, None, None, None] for part in jnp.split(own, 4, axis=1)]
    for step in range(4):
        parts = lax.optimization_barrier(parts)
        others = [
            swap(part, "cand", 16, CAND_MASKS[order[step]])
            for part, order in zip(parts, PART_ORDERS)
        ]
        others = lax.optimization_barrier(others)
        merged = []
        for part, other, order in zip(parts, others, PART_ORDERS):
            bit = bits[order[step]]
            low = jnp.where(bit == 0, part, other)
            high = jnp.where(bit == 0, other, part)
            merged.append(jnp.concatenate([low, high], axis=3 - order[step]))
        parts = merged
    return parts


def sum_goals(terms, core, low_bit, high_bit):
    blocks = terms.reshape(terms.shape[0], 4, 2, 512, 256)
    send = jnp.where(core == 0, blocks[:, :, 1], blocks[:, :, 0])
    keep = jnp.where(core == 0, blocks[:, :, 0], blocks[:, :, 1])
    both = plus(keep, swap(send, "goal", 8, 1))
    halves = []
    for part, first in ((both[:, :, :256], 0), (both[:, :, 256:], 1)):
        lines = jnp.stack([part[:, 0], part[:, 1], part[:, 3], part[:, 2]], axis=1)
        lines = lines.reshape(terms.shape[0], 2, 2, 256, 256)
        halves.append((lines, first))
    bits = (low_bit, high_bit)
    masks = (2, 6)
    kept = []
    for lines, first in halves:
        zero, one = (lines[:, :, 0], lines[:, :, 1]) if first == 0 else (lines[:, 0], lines[:, 1])
        bit = bits[first]
        other = swap(jnp.where(bit == 0, one, zero), "goal", 8, masks[first])
        kept.append(plus(jnp.where(bit == 0, zero, one), other))
    done = []
    for lines, second in zip(kept, (1, 0)):
        zero, one = lines[:, 0], lines[:, 1]
        bit = bits[second]
        other = swap(jnp.where(bit == 0, one, zero), "goal", 8, masks[second])
        done.append(plus(jnp.where(bit == 0, zero, one), other))
    return jnp.concatenate(done, axis=1)


def plus(left, right):
    return (left.astype(jnp.float32) + right.astype(jnp.float32)).astype(jnp.bfloat16)


def rounded(values):
    return lax.optimization_barrier(values.astype(jnp.bfloat16)).astype(jnp.float32)


def attend(query, key, value, heads_here):
    total_rows = query.shape[0]
    memory_rows = key.shape[0]
    query_heads = query.reshape(total_rows, heads_here, HD)
    key_heads = key.reshape(memory_rows, heads_here, HD)
    value_heads = value.reshape(memory_rows, heads_here, HD)
    scores = jnp.einsum(
        "rhe,mhe->hrm", query_heads, key_heads, preferred_element_type=jnp.float32
    ) * HD ** (-0.5)
    softmaxed = jax.nn.softmax(scores, axis=-1)
    softmaxed_low = softmaxed.astype(jnp.bfloat16)
    mixed = jnp.einsum(
        "hrm,mhe->rhe", softmaxed_low, value_heads, preferred_element_type=jnp.float32
    )
    return (
        mixed.astype(jnp.bfloat16).reshape(total_rows, heads_here * HD),
        softmaxed,
        softmaxed_low,
    )


def token_terms(rows, attended, weighted):
    hidden = rows.astype(jnp.float32) + attended
    inverse = lax.rsqrt(jnp.mean(hidden * hidden, axis=-1) + 1e-06)
    raw = jnp.sum(hidden * weighted[None, :], axis=-1)
    return (hidden, inverse, raw)


def goal_softmax(logits, live, visit):
    masked = jnp.where(live, logits, -1e30)
    top_value = jnp.max(masked)
    exponent = jnp.where(live, jnp.exp(masked - top_value), 0.0)
    log_total = top_value + jnp.log(jnp.sum(exponent))
    log_weight = jnp.where(live, logits - log_total, 0.0)
    visit_mass = jnp.where(live, visit.astype(jnp.float32), 0.0)
    target = visit_mass / jnp.sum(visit_mass)
    loss = -jnp.sum(target * log_weight)
    logit_grad = jnp.where(live, jnp.exp(log_weight) - target, 0.0)
    return (log_weight, loss, logit_grad)


def norm_grad(hidden, inverse, raw, tok_grad, weighted, model_width):
    factor = inverse * inverse * inverse * tok_grad * raw / model_width
    return ((inverse * tok_grad)[:, None] * weighted[None, :] - hidden * factor[:, None]).astype(
        jnp.bfloat16
    )


def body(dec_states, memory, counts, rank, visits, w_query, w_key, w_value, w_out, gain, w_score):
    width = w_query.shape[1]
    model_width = w_query.shape[0]
    heads_here = width // HD
    slot_here = dec_states.shape[1]
    cand = lax.axis_index("cand")
    goal = lax.axis_index("goal")
    bits = pair_bits(cand >> 2) + pair_bits(cand & 3)
    per_tactic = dec_states.shape[2]
    own_rows = slot_here * per_tactic
    own = jnp.concatenate([dec_states[0].reshape(own_rows, model_width), memory[0]], axis=0)
    parts = gather_cand(own, bits)
    slots = 16 * slot_here
    rows = jnp.concatenate(
        [part[..., :own_rows, :].reshape(16 * own_rows, -1) for part in parts], axis=1
    )
    memory_all = jnp.concatenate(
        [part[..., own_rows:, :].reshape(16 * memory.shape[1], -1) for part in parts], axis=1
    )
    order = jnp.array([c * slot_here + s for c in slot_order() for s in range(slot_here)], jnp.int32)
    pick = order[:, None] == jnp.arange(slots, dtype=jnp.int32)[None, :]
    rank_here = jnp.sum(jnp.where(pick, rank, 0), axis=1)
    visits_here = jnp.sum(jnp.where(pick, visits, 0), axis=1)
    total_rows = rows.shape[0]
    memory_rows = memory_all.shape[0]
    query = jnp.dot(rows, w_query, preferred_element_type=jnp.float32).astype(jnp.bfloat16)
    key = jnp.dot(memory_all, w_key, preferred_element_type=jnp.float32).astype(jnp.bfloat16)
    value = jnp.dot(memory_all, w_value, preferred_element_type=jnp.float32).astype(jnp.bfloat16)
    mixed, softmaxed, softmaxed_low = attend(query, key, value, heads_here)
    weighted = gain * w_score
    live = rank_here < counts[0]
    own_part = rounded(jnp.dot(mixed, w_out, preferred_element_type=jnp.float32))
    attended = lax.psum(own_part.astype(jnp.bfloat16), "cand").astype(jnp.float32)
    hidden, inverse, raw = token_terms(rows, attended, weighted)
    logits = jnp.mean((inverse * raw).reshape(slots, per_tactic), axis=1)
    log_weight, loss, logit_grad = goal_softmax(logits, live, visits_here)
    tok_grad = jnp.repeat(logit_grad / per_tactic, per_tactic, total_repeat_length=total_rows)
    hidden_grad = norm_grad(hidden, inverse, raw, tok_grad, weighted, model_width)
    mixed_grad = lax.dot_general(
        hidden_grad, w_out, (((1,), (1,)), ((), ())), preferred_element_type=jnp.float32
    ).astype(jnp.bfloat16)
    out_term = lax.dot_general(
        hidden_grad, mixed, (((0,), (0,)), ((), ())), preferred_element_type=jnp.float32
    )
    query_heads = query.reshape(total_rows, heads_here, HD)
    key_heads = key.reshape(memory_rows, heads_here, HD)
    value_heads = value.reshape(memory_rows, heads_here, HD)
    grad_heads = mixed_grad.reshape(total_rows, heads_here, HD)
    prob_grad = jnp.einsum(
        "rhe,mhe->hrm", grad_heads, value_heads, preferred_element_type=jnp.float32
    )
    delta = jnp.sum(softmaxed * prob_grad, axis=-1, keepdims=True)
    score_grad = (softmaxed * (prob_grad - delta) * HD ** (-0.5)).astype(jnp.bfloat16)
    query_grad = jnp.einsum(
        "hrm,mhe->rhe", score_grad, key_heads, preferred_element_type=jnp.float32
    )
    query_grad = query_grad.astype(jnp.bfloat16).reshape(total_rows, width)
    key_grad = jnp.einsum(
        "hrm,rhe->mhe", score_grad, query_heads, preferred_element_type=jnp.float32
    )
    key_grad = key_grad.astype(jnp.bfloat16).reshape(memory_rows, width)
    value_grad = jnp.einsum(
        "hrm,rhe->mhe", softmaxed_low, grad_heads, preferred_element_type=jnp.float32
    )
    value_grad = value_grad.astype(jnp.bfloat16).reshape(memory_rows, width)
    contract = (((0,), (0,)), ((), ()))
    query_term = lax.dot_general(rows, query_grad, contract, preferred_element_type=jnp.float32)
    key_term = lax.dot_general(memory_all, key_grad, contract, preferred_element_type=jnp.float32)
    value_term = lax.dot_general(
        memory_all, value_grad, contract, preferred_element_type=jnp.float32
    )
    core = goal & 1
    low_bit, high_bit = pair_bits(goal >> 1)
    first = jnp.stack([out_term.astype(jnp.bfloat16), value_term.astype(jnp.bfloat16)])
    second = jnp.stack([query_term.astype(jnp.bfloat16), key_term.astype(jnp.bfloat16)])
    first = sum_goals(first, core, low_bit, high_bit)
    second = sum_goals(second, core, low_bit, high_bit)
    own_slots = cand * slot_here + jnp.arange(slot_here, dtype=jnp.int32)
    own_log = jnp.sum(jnp.where(own_slots[:, None] == order[None, :], log_weight[None, :], 0.0), axis=1)
    return (
        own_log[None, :],
        loss[None],
        second[0],
        second[1],
        first[1],
        first[0].T,
    )


def solution(mesh):
    return jax.shard_map(
        body,
        mesh=mesh,
        in_specs=(
            P("goal", "cand", None, None),
            P("goal", "cand", None),
            P("goal"),
            P("goal", None),
            P("goal", None),
            P(None, "cand"),
            P(None, "cand"),
            P(None, "cand"),
            P("cand", None),
            P(),
            P(),
        ),
        out_specs=(
            P("goal", "cand"),
            P("goal"),
            P("goal", "cand"),
            P("goal", "cand"),
            P("goal", "cand"),
            P("cand", "goal"),
        ),
        check_vma=False,
    )
```

```python
import jax
import jax.numpy as jnp
from jax import lax
from jax.experimental import pallas as pl
from jax.experimental.pallas import tpu as pltpu
from jax.sharding import PartitionSpec as P

HD = 64
HEADS_HERE = 4
TOKEN_BLOCK = 256
X_MASKS = (4, 12)
Y_MASKS = (1, 3)
CAND_MASKS = X_MASKS + Y_MASKS
GOAL_MASKS = (2, 6)
PART_ORDERS = ((0, 1, 2, 3), (1, 0, 3, 2), (2, 3, 0, 1), (3, 2, 1, 0))
SUM_ROWS = (((0,), (0,)), ((), ()))
SUM_COLUMNS = (((1,), (1,)), ((), ()))


def swap_cand(values, mask):
    return lax.ppermute(values, "cand", [(i, i ^ mask) for i in range(16)])


def swap_goal(values, mask):
    return lax.ppermute(values, "goal", [(i, i ^ mask) for i in range(8)])


def plus(left, right):
    return left.astype(jnp.float32) + right.astype(jnp.float32)


def low(values):
    return values.astype(jnp.bfloat16)


def pair_bits(coordinate):
    high = coordinate >> 1
    return ((coordinate & 1) ^ high, high)


def cand_order():
    order = []
    for position in range(16):
        bits = [(position >> i) & 1 for i in range(4)]
        order.append(4 * (bits[0] ^ (3 * bits[1])) + (bits[2] ^ (3 * bits[3])))
    return order


def gather_cand(own, bits):
    parts = [part[None, None, None, None] for part in jnp.split(own, 4, axis=1)]
    for step in range(4):
        parts = lax.optimization_barrier(parts)
        others = [
            swap_cand(part, CAND_MASKS[order[step]]) for part, order in zip(parts, PART_ORDERS)
        ]
        others = lax.optimization_barrier(others)
        merged = []
        for part, other, order in zip(parts, others, PART_ORDERS):
            bit = bits[order[step]]
            first = jnp.where(bit == 0, part, other)
            second = jnp.where(bit == 0, other, part)
            merged.append(jnp.concatenate([first, second], axis=3 - order[step]))
        parts = merged
    return parts


def spread_out_weights(w_out, y, core):
    height, width = w_out.shape[0] // 2, w_out.shape[1] // 4

    def half_block(index):
        return lax.dynamic_slice(w_out, (core * height, index * width), (height, width))

    got = jnp.concatenate([swap_cand(half_block(y ^ mask), mask) for mask in (1, 3, 2)], axis=0)
    other = swap_goal(got, 1)
    first = jnp.where(core == 0, got, other).reshape(3, height, width)
    second = jnp.where(core == 0, other, got).reshape(3, height, width)
    received = jnp.stack([first, second], axis=1).reshape(6 * height, width)
    own = lax.dynamic_slice_in_dim(w_out, y * width, width, 1)
    return jnp.concatenate([own, received], axis=0)


def gather_heads(mixed):
    halves = jnp.split(mixed, 2, axis=0)
    near = [swap_cand(half, mask) for half, mask in zip(halves, Y_MASKS)]
    pairs = [jnp.concatenate([half, other], axis=1) for half, other in zip(halves, near)]
    far = [swap_cand(pair, mask) for pair, mask in zip(pairs, Y_MASKS[::-1])]
    width = mixed.shape[1]
    second = jnp.concatenate(
        [halves[1], far[1][:, :width], near[1], far[1][:, width:]], axis=1
    )
    first = jnp.concatenate([halves[0], near[0], far[0]], axis=1)
    return jnp.concatenate([first, second], axis=0)


def sum_line(values):
    parts = jnp.split(low(values), 2, axis=1)
    for masks in (X_MASKS, X_MASKS[::-1]):
        others = [swap_cand(part, mask) for part, mask in zip(parts, masks)]
        totals = [plus(part, other) for part, other in zip(parts, others)]
        parts = [low(total) for total in totals]
    return jnp.concatenate(totals, axis=1)


def scatter_heads(values, width):
    halves = jnp.split(low(values), 2, axis=0)
    blocks = [[half[:, i * width : (i + 1) * width] for i in range(4)] for half in halves]
    keep = [jnp.concatenate(blocks[0][:2], axis=1), jnp.concatenate(blocks[1][::2], axis=1)]
    send = [jnp.concatenate(blocks[0][2:], axis=1), jnp.concatenate(blocks[1][1::2], axis=1)]
    others = [swap_cand(part, mask) for part, mask in zip(send, Y_MASKS[::-1])]
    kept = [low(plus(part, other)) for part, other in zip(keep, others)]
    others = [swap_cand(part[:, width:], mask) for part, mask in zip(kept, Y_MASKS)]
    return jnp.concatenate(
        [plus(part[:, :width], other) for part, other in zip(kept, others)], axis=0
    )


def sum_goals(lines, core, bits):
    send = jnp.where(core == 0, lines[:, :, 1], lines[:, :, 0])
    keep = jnp.where(core == 0, lines[:, :, 0], lines[:, :, 1])
    both = low(plus(keep, swap_goal(send, 1)))
    count, _, height, width = both.shape
    both = both.reshape(count, 2, 2, height, width)
    parts = [both[:, :, :, : height // 2], both[:, :, :, height // 2 :]]
    zeros = [parts[0][:, :, 0], parts[1][:, 0]]
    ones = [parts[0][:, :, 1], parts[1][:, 1]]
    for turn in (0, 1):
        which = (turn, 1 - turn)
        sends = [jnp.where(bits[w] == 0, one, zero) for w, zero, one in zip(which, zeros, ones)]
        keeps = [jnp.where(bits[w] == 0, zero, one) for w, zero, one in zip(which, zeros, ones)]
        others = [swap_goal(part, GOAL_MASKS[w]) for part, w in zip(sends, which)]
        sums = [low(plus(part, other)) for part, other in zip(keeps, others)]
        zeros = [part[:, 0] for part in sums]
        ones = [part[:, 1] for part in sums]
    return jnp.concatenate(sums, axis=1)


def row_lines(term):
    blocks = low(term).reshape(4, 2, -1, term.shape[1])
    return jnp.stack([blocks[0], blocks[1], blocks[3], blocks[2]])[None]


def head_mask(head, dtype):
    lane = lax.broadcasted_iota(jnp.int32, (1, HEADS_HERE * HD), 1)
    inside = (lane >= head * HD) & (lane < (head + 1) * HD)
    return jnp.where(inside, 1.0, 0.0).astype(dtype)


def attend_kernel(query_ref, key_ref, value_ref, mixed_ref, prob_ref, flipped_ref):
    @pl.when(pl.program_id(0) == 0)
    def _():
        flipped_ref[...] = value_ref[...].astype(jnp.float32).T.astype(jnp.bfloat16)

    query = query_ref[...] * jnp.bfloat16(HD ** (-0.5))
    key = key_ref[...]
    outs = []
    for head in range(HEADS_HERE):
        scores = matmul(key * head_mask(head, jnp.bfloat16), query, SUM_COLUMNS)
        exponent = jnp.exp(scores - jnp.max(scores, axis=0, keepdims=True))
        share = 1.0 / jnp.sum(exponent, axis=0, keepdims=True)
        prob = (exponent * share).astype(jnp.bfloat16)
        prob_ref[head] = prob
        outs.append(matmul(flipped_ref[head * HD : (head + 1) * HD, :], prob))
    mixed_ref[...] = jnp.concatenate(outs, axis=0).T.astype(jnp.bfloat16)


def attend(query, key, value):
    tokens, width = query.shape
    memory_rows = key.shape[0]
    whole = pl.BlockSpec((memory_rows, width), lambda i: (0, 0))
    block = pl.BlockSpec((TOKEN_BLOCK, width), lambda i: (i, 0))
    return pl.pallas_call(
        attend_kernel,
        grid=(tokens // TOKEN_BLOCK,),
        in_specs=[block, whole, whole],
        out_specs=[
            block,
            pl.BlockSpec((HEADS_HERE, memory_rows, TOKEN_BLOCK), lambda i: (0, 0, i)),
        ],
        out_shape=[
            jax.ShapeDtypeStruct((tokens, width), jnp.bfloat16),
            jax.ShapeDtypeStruct((HEADS_HERE, memory_rows, tokens), jnp.bfloat16),
        ],
        scratch_shapes=[pltpu.VMEM((width, memory_rows), jnp.bfloat16)],
        compiler_params=pltpu.CompilerParams(vmem_limit_bytes=24 * 1024 * 1024),
        name="attend",
    )(query, key, value)


def attend_grads_kernel(
    query_ref,
    key_ref,
    value_ref,
    prob_ref,
    hidden_out_ref,
    coefficient_ref,
    score_out_ref,
    query_grad_ref,
    key_grad_ref,
    value_grad_ref,
    flipped_ref,
    key_sum_ref,
    value_sum_ref,
):
    step = pl.program_id(0)

    @pl.when(step == 0)
    def _():
        flipped_ref[...] = key_ref[...].astype(jnp.float32).T.astype(jnp.bfloat16)
        key_sum_ref[...] = jnp.zeros_like(key_sum_ref)
        value_sum_ref[...] = jnp.zeros_like(value_sum_ref)

    coefficient = coefficient_ref[...]
    mixed_grad = coefficient[:, 0:1] * score_out_ref[...] - coefficient[:, 1:2] * hidden_out_ref[...]
    mixed_grad = mixed_grad.astype(jnp.bfloat16)
    query = query_ref[...]
    value = value_ref[...]
    outs = []
    key_sum = key_sum_ref[...]
    value_sum = value_sum_ref[...]
    for head in range(HEADS_HERE):
        prob_grad = matmul(value * head_mask(head, jnp.bfloat16), mixed_grad, SUM_COLUMNS)
        prob_low = prob_ref[head]
        prob = prob_low.astype(jnp.float32)
        delta = jnp.sum(prob * prob_grad, axis=0, keepdims=True)
        score_grad = (prob * ((prob_grad - delta) * HD ** (-0.5))).astype(jnp.bfloat16)
        mask = head_mask(head, jnp.float32)
        key_sum = key_sum + matmul(score_grad, query) * mask
        value_sum = value_sum + matmul(prob_low, mixed_grad) * mask
        outs.append(matmul(flipped_ref[head * HD : (head + 1) * HD, :], score_grad))
    key_sum_ref[...] = key_sum
    value_sum_ref[...] = value_sum
    query_grad_ref[...] = jnp.concatenate(outs, axis=0).T.astype(jnp.bfloat16)

    @pl.when(step == pl.num_programs(0) - 1)
    def _():
        key_grad_ref[...] = key_sum_ref[...].astype(jnp.bfloat16)
        value_grad_ref[...] = value_sum_ref[...].astype(jnp.bfloat16)


def attend_grads(query, key, value, prob, hidden_out, coefficient, score_out):
    tokens, width = query.shape
    memory_rows = key.shape[0]
    whole = pl.BlockSpec((memory_rows, width), lambda i: (0, 0))
    block = pl.BlockSpec((TOKEN_BLOCK, width), lambda i: (i, 0))
    return pl.pallas_call(
        attend_grads_kernel,
        grid=(tokens // TOKEN_BLOCK,),
        in_specs=[
            block,
            whole,
            whole,
            pl.BlockSpec((HEADS_HERE, memory_rows, TOKEN_BLOCK), lambda i: (0, 0, i)),
            block,
            pl.BlockSpec((TOKEN_BLOCK, 2), lambda i: (i, 0)),
            pl.BlockSpec((1, width), lambda i: (0, 0)),
        ],
        out_specs=[block, whole, whole],
        out_shape=[
            jax.ShapeDtypeStruct((tokens, width), jnp.bfloat16),
            jax.ShapeDtypeStruct((memory_rows, width), jnp.bfloat16),
            jax.ShapeDtypeStruct((memory_rows, width), jnp.bfloat16),
        ],
        scratch_shapes=[
            pltpu.VMEM((width, memory_rows), jnp.bfloat16),
            pltpu.VMEM((memory_rows, width), jnp.float32),
            pltpu.VMEM((memory_rows, width), jnp.float32),
        ],
        compiler_params=pltpu.CompilerParams(vmem_limit_bytes=24 * 1024 * 1024),
        name="attend_grads",
    )(query, key, value, prob, hidden_out, coefficient, score_out)


def head_kernel(
    counts_ref,
    sums_ref,
    hidden_ref,
    weighted_ref,
    rank_ref,
    visits_ref,
    hidden_grad_ref,
    coefficient_ref,
    log_ref,
    loss_ref,
):
    tokens, slots = sums_ref.shape[0], rank_ref.shape[1]
    per_tactic = tokens // slots
    model_width = 4 * hidden_ref.shape[1]
    inverse = lax.rsqrt(sums_ref[:, 0:1] / model_width + 1e-06)
    raw = sums_ref[:, 1:2]
    token = lax.broadcasted_iota(jnp.int32, (tokens, slots), 0)
    first = lax.broadcasted_iota(jnp.int32, (tokens, slots), 1) * per_tactic
    member = (token >= first) & (token < first + per_tactic)
    logits = jnp.sum(jnp.where(member, inverse * raw, 0.0), axis=0, keepdims=True) / per_tactic
    live = rank_ref[...] < counts_ref[0]
    masked = jnp.where(live, logits, -1e30)
    top_value = jnp.max(masked, axis=1, keepdims=True)
    exponent = jnp.where(live, jnp.exp(masked - top_value), 0.0)
    log_total = top_value + jnp.log(jnp.sum(exponent, axis=1, keepdims=True))
    log_weight = jnp.where(live, logits - log_total, 0.0)
    visit_mass = jnp.where(live, visits_ref[...].astype(jnp.float32), 0.0)
    target = visit_mass / jnp.sum(visit_mass, axis=1, keepdims=True)
    log_ref[...] = log_weight
    loss_ref[...] = -jnp.sum(target * log_weight, axis=1, keepdims=True)
    logit_grad = jnp.where(live, jnp.exp(log_weight) - target, 0.0) / per_tactic
    tok_grad = jnp.sum(jnp.where(member, logit_grad, 0.0), axis=1, keepdims=True)
    near = inverse * tok_grad
    far = inverse * inverse * inverse * tok_grad * raw / model_width
    hidden_grad_ref[...] = (near * weighted_ref[...] - hidden_ref[...] * far).astype(jnp.bfloat16)
    coefficient_ref[:, 0:1] = near
    coefficient_ref[:, 1:2] = far


def policy_head(counts, sums, hidden, weighted, rank, visits):
    in_vmem = pl.BlockSpec(memory_space=pltpu.VMEM)
    tokens, width = hidden.shape
    slots = rank.shape[1]
    return pl.pallas_call(
        head_kernel,
        in_specs=[pl.BlockSpec(memory_space=pltpu.SMEM)] + [in_vmem] * 5,
        out_specs=[in_vmem] * 4,
        out_shape=[
            jax.ShapeDtypeStruct((tokens, width), jnp.bfloat16),
            jax.ShapeDtypeStruct((tokens, 2), jnp.float32),
            jax.ShapeDtypeStruct((1, slots), jnp.float32),
            jax.ShapeDtypeStruct((1, 1), jnp.float32),
        ],
        compiler_params=pltpu.CompilerParams(vmem_limit_bytes=16 * 1024 * 1024),
        name="policy_head",
    )(counts, sums, hidden, weighted, rank, visits)


def matmul(left, right, contract=(((1,), (0,)), ((), ()))):
    return lax.dot_general(left, right, contract, preferred_element_type=jnp.float32)


def body(dec_states, memory, counts, rank, visits, w_query, w_key, w_value, w_out, gain, w_score):
    model_width, width = w_query.shape
    slot_here, per_tactic = dec_states.shape[1:3]
    own_rows = slot_here * per_tactic
    slots = 16 * slot_here
    total_rows = slots * per_tactic
    slice_width = model_width // 4
    cand = lax.axis_index("cand")
    goal = lax.axis_index("goal")
    y = cand & 3
    core = goal & 1
    goal_bits = pair_bits(goal >> 1)

    own = jnp.concatenate([dec_states[0].reshape(own_rows, model_width), memory[0]], axis=0)
    parts = gather_cand(own, pair_bits(cand >> 2) + pair_bits(y))
    rows = jnp.concatenate(
        [part[..., :own_rows, :].reshape(total_rows, -1) for part in parts], axis=1
    )
    memory_all = jnp.concatenate(
        [part[..., own_rows:, :].reshape(16 * memory.shape[1], -1) for part in parts], axis=1
    )
    rows, memory_all, w_out = lax.optimization_barrier((rows, memory_all, w_out))
    w_slice = spread_out_weights(w_out, y, core)

    query = low(matmul(rows, w_query))
    key = low(matmul(memory_all, w_key))
    value = low(matmul(memory_all, w_value))
    mixed, prob = attend(query, key, value)

    weighted = gain * w_score
    score_out = jnp.sum(w_out.astype(jnp.float32) * weighted[None, :], axis=1)
    order = jnp.array([c * slot_here + s for c in cand_order() for s in range(slot_here)], jnp.int32)
    pick = order[None, :] == jnp.arange(slots, dtype=jnp.int32)[:, None]
    rank_here = jnp.sum(jnp.where(pick, rank[0][:, None], 0), axis=0, keepdims=True)
    visits_here = jnp.sum(jnp.where(pick, visits[0][:, None], 0), axis=0, keepdims=True)

    mixed_line = gather_heads(mixed)
    attended = sum_line(matmul(mixed_line, w_slice))
    hidden = lax.dynamic_slice_in_dim(rows, y * slice_width, slice_width, 1).astype(jnp.float32)
    hidden = hidden + attended
    weighted_slice = lax.dynamic_slice_in_dim(weighted, y * slice_width, slice_width, 0)
    sums = jnp.stack([jnp.sum(hidden * hidden, axis=1), jnp.sum(hidden * weighted_slice, axis=1)])
    hidden_out = scatter_heads(matmul(low(hidden), w_slice, SUM_COLUMNS), width)
    for mask in Y_MASKS:
        sums = sums + swap_cand(sums, mask)
    hidden_grad, coefficient, log_weight, loss = policy_head(
        counts, sums.T, hidden, weighted_slice[None, :], rank_here, visits_here
    )

    half = slice_width // 2
    out_term = jnp.concatenate(
        [
            low(matmul(mixed_line, hidden_grad[:, side * half : (side + 1) * half], SUM_ROWS))
            for side in (0, 1)
        ],
        axis=0,
    )
    grad_out = lax.psum_scatter(out_term, "goal", scatter_dimension=0, tiled=True)
    pairs = []
    for g in range(8):
        for c in range(16):
            goal_to = 2 * (c & 3) + (g >> 2)
            pairs.append((16 * g + c, 16 * goal_to + (c ^ (0, 1, 3, 2)[g & 3])))
    grad_out = lax.ppermute(grad_out, ("goal", "cand"), pairs)

    query_grad, key_grad, value_grad = attend_grads(
        query, key, value, prob, hidden_out, coefficient, score_out[None, :]
    )
    value_term = low(matmul(memory_all, value_grad, SUM_ROWS))
    grad_value = lax.psum_scatter(value_term, "goal", scatter_dimension=0, tiled=True)
    query_lines = row_lines(matmul(rows, query_grad, SUM_ROWS))
    key_lines = row_lines(matmul(memory_all, key_grad, SUM_ROWS))
    grad_both = sum_goals(jnp.concatenate([query_lines, key_lines]), core, goal_bits)
    own_slots = cand * slot_here + jnp.arange(slot_here, dtype=jnp.int32)
    own_log = jnp.sum(
        jnp.where(own_slots[:, None] == order[None, :], log_weight, 0.0), axis=1
    )
    return own_log[None, :], loss[0], grad_both[0], grad_both[1], grad_value, grad_out


def solution(mesh):
    return jax.shard_map(
        body,
        mesh=mesh,
        in_specs=(
            P("goal", "cand", None, None),
            P("goal", "cand", None),
            P("goal"),
            P("goal", None),
            P("goal", None),
            P(None, "cand"),
            P(None, "cand"),
            P(None, "cand"),
            P("cand", None),
            P(),
            P(),
        ),
        out_specs=(
            P("goal", "cand"),
            P("goal"),
            P("goal", "cand"),
            P("goal", "cand"),
            P("goal", "cand"),
            P("cand", "goal"),
        ),
        check_vma=False,
    )
```

```python
import jax
import jax.numpy as jnp
from jax import lax
from jax.experimental import pallas as pl
from jax.experimental.pallas import tpu as pltpu
from jax.sharding import PartitionSpec as P

HD = 64
HEADS_HERE = 4
TOKEN_BLOCK = 256
X_MASKS = (4, 12)
Y_MASKS = (1, 3)
CAND_MASKS = X_MASKS + Y_MASKS
GOAL_MASKS = (2, 6)
PART_ORDERS = ((0, 1, 2, 3), (1, 0, 3, 2), (2, 3, 0, 1), (3, 2, 1, 0))
SUM_ROWS = (((0,), (0,)), ((), ()))
SUM_COLUMNS = (((1,), (1,)), ((), ()))


def swap_cand(values, mask):
    return lax.ppermute(values, "cand", [(i, i ^ mask) for i in range(16)])


def swap_goal(values, mask):
    return lax.ppermute(values, "goal", [(i, i ^ mask) for i in range(8)])


def exchange(parts, masks, swap=swap_cand):
    parts = lax.optimization_barrier(list(parts))
    return lax.optimization_barrier([swap(part, mask) for part, mask in zip(parts, masks)])


def plus(left, right):
    return left.astype(jnp.float32) + right.astype(jnp.float32)


def low(values):
    return values.astype(jnp.bfloat16)


def pair_bits(coordinate):
    high = coordinate >> 1
    return ((coordinate & 1) ^ high, high)


def cand_order():
    order = []
    for position in range(16):
        bits = [(position >> i) & 1 for i in range(4)]
        order.append(4 * (bits[0] ^ (3 * bits[1])) + (bits[2] ^ (3 * bits[3])))
    return order


def gather_cand(own, bits):
    parts = [part[None, None, None, None] for part in jnp.split(own, 4, axis=1)]
    for step in range(4):
        others = exchange(parts, [CAND_MASKS[order[step]] for order in PART_ORDERS])
        merged = []
        for part, other, order in zip(parts, others, PART_ORDERS):
            bit = bits[order[step]]
            first = jnp.where(bit == 0, part, other)
            second = jnp.where(bit == 0, other, part)
            merged.append(jnp.concatenate([first, second], axis=3 - order[step]))
        parts = merged
    return parts


def spread_out_weights(w_out, y, core):
    height, width = w_out.shape[0] // 2, w_out.shape[1] // 4

    def half_block(index):
        return lax.dynamic_slice(w_out, (core * height, index * width), (height, width))

    got = jnp.concatenate(exchange([half_block(y ^ mask) for mask in (1, 3, 2)], (1, 3, 2)), axis=0)
    other = swap_goal(got, 1)
    first = jnp.where(core == 0, got, other).reshape(3, height, width)
    second = jnp.where(core == 0, other, got).reshape(3, height, width)
    received = jnp.stack([first, second], axis=1).reshape(6 * height, width)
    own = lax.dynamic_slice_in_dim(w_out, y * width, width, 1)
    return jnp.concatenate([own, received], axis=0)


def gather_heads(mixed):
    halves = jnp.split(mixed, 2, axis=0)
    near = exchange(halves, Y_MASKS)
    pairs = [jnp.concatenate([half, other], axis=1) for half, other in zip(halves, near)]
    far = exchange(pairs, Y_MASKS[::-1])
    width = mixed.shape[1]
    second = jnp.concatenate(
        [halves[1], far[1][:, :width], near[1], far[1][:, width:]], axis=1
    )
    first = jnp.concatenate([halves[0], near[0], far[0]], axis=1)
    return jnp.concatenate([first, second], axis=0)


def sum_line(values):
    parts = jnp.split(low(values), 2, axis=1)
    for masks in (X_MASKS, X_MASKS[::-1]):
        others = exchange(parts, masks)
        totals = [plus(part, other) for part, other in zip(parts, others)]
        parts = [low(total) for total in totals]
    return jnp.concatenate(totals, axis=1)


def scatter_heads_start(values, width):
    halves = jnp.split(low(values), 2, axis=0)
    blocks = [[half[:, i * width : (i + 1) * width] for i in range(4)] for half in halves]
    keep = [jnp.concatenate(blocks[0][:2], axis=1), jnp.concatenate(blocks[1][::2], axis=1)]
    send = [jnp.concatenate(blocks[0][2:], axis=1), jnp.concatenate(blocks[1][1::2], axis=1)]
    others = exchange(send, Y_MASKS[::-1])
    return [low(plus(part, other)) for part, other in zip(keep, others)]


def scatter_heads_end(kept, width):
    others = exchange([part[:, width:] for part in kept], Y_MASKS)
    return jnp.concatenate(
        [plus(part[:, :width], other) for part, other in zip(kept, others)], axis=0
    )


def core_halves(values, core):
    half = values.shape[1] // 2
    left, right = values[:, :half], values[:, half:]
    return jnp.where(core == 0, left, right), jnp.where(core == 0, right, left)


def both_cores(values):
    return jnp.concatenate([values, swap_goal(values, 1)], axis=0)


def share_columns(values, core):
    quarters = [core_halves(part, core) for part in jnp.split(values, 4, axis=1)]
    quarters = [quarters[i] for i in (0, 1, 3, 2)]
    keep = jnp.concatenate([quarter[0] for quarter in quarters], axis=1)
    send = jnp.concatenate([quarter[1] for quarter in quarters], axis=1)
    return jnp.concatenate([keep, swap_goal(send, 1)], axis=0)


def sum_z(lines, bits):
    count, _, height, width = lines.shape
    lines = lines.reshape(count, 2, 2, height, width)
    parts = [lines[:, :, :, : height // 2], lines[:, :, :, height // 2 :]]
    zeros = [parts[0][:, :, 0], parts[1][:, 0]]
    ones = [parts[0][:, :, 1], parts[1][:, 1]]
    for turn in (0, 1):
        which = (turn, 1 - turn)
        sends = [jnp.where(bits[w] == 0, one, zero) for w, zero, one in zip(which, zeros, ones)]
        keeps = [jnp.where(bits[w] == 0, zero, one) for w, zero, one in zip(which, zeros, ones)]
        others = exchange(sends, [GOAL_MASKS[w] for w in which], swap_goal)
        sums = [low(plus(part, other)) for part, other in zip(keeps, others)]
        zeros = [part[:, 0] for part in sums]
        ones = [part[:, 1] for part in sums]
    return jnp.concatenate(sums, axis=1)


def head_mask(head, dtype):
    lane = lax.broadcasted_iota(jnp.int32, (1, HEADS_HERE * HD), 1)
    inside = (lane >= head * HD) & (lane < (head + 1) * HD)
    return jnp.where(inside, 1.0, 0.0).astype(dtype)


def attend_kernel(query_ref, key_ref, value_ref, mixed_ref, prob_ref, flipped_ref):
    @pl.when(pl.program_id(0) == 0)
    def _():
        flipped_ref[...] = value_ref[...].astype(jnp.float32).T.astype(jnp.bfloat16)

    query = query_ref[...] * jnp.bfloat16(HD ** (-0.5))
    key = key_ref[...]
    outs = []
    for head in range(HEADS_HERE):
        scores = matmul(key * head_mask(head, jnp.bfloat16), query, SUM_COLUMNS)
        exponent = jnp.exp(scores - jnp.max(scores, axis=0, keepdims=True))
        share = 1.0 / jnp.sum(exponent, axis=0, keepdims=True)
        prob = (exponent * share).astype(jnp.bfloat16)
        prob_ref[head] = prob
        outs.append(matmul(flipped_ref[head * HD : (head + 1) * HD, :], prob))
    mixed_ref[...] = jnp.concatenate(outs, axis=0).T.astype(jnp.bfloat16)


def attend(query, key, value):
    tokens, width = query.shape
    memory_rows = key.shape[0]
    whole = pl.BlockSpec((memory_rows, width), lambda i: (0, 0))
    block = pl.BlockSpec((TOKEN_BLOCK, width), lambda i: (i, 0))
    return pl.pallas_call(
        attend_kernel,
        grid=(tokens // TOKEN_BLOCK,),
        in_specs=[block, whole, whole],
        out_specs=[
            block,
            pl.BlockSpec((HEADS_HERE, memory_rows, TOKEN_BLOCK), lambda i: (0, 0, i)),
        ],
        out_shape=[
            jax.ShapeDtypeStruct((tokens, width), jnp.bfloat16),
            jax.ShapeDtypeStruct((HEADS_HERE, memory_rows, tokens), jnp.bfloat16),
        ],
        scratch_shapes=[pltpu.VMEM((width, memory_rows), jnp.bfloat16)],
        compiler_params=pltpu.CompilerParams(vmem_limit_bytes=24 * 1024 * 1024),
        name="attend",
    )(query, key, value)


def attend_grads_kernel(
    query_ref,
    key_ref,
    value_ref,
    prob_ref,
    hidden_out_ref,
    coefficient_ref,
    score_out_ref,
    query_grad_ref,
    key_grad_ref,
    value_grad_ref,
    flipped_ref,
    key_sum_ref,
    value_sum_ref,
):
    step = pl.program_id(0)

    @pl.when(step == 0)
    def _():
        flipped_ref[...] = key_ref[...].astype(jnp.float32).T.astype(jnp.bfloat16)
        key_sum_ref[...] = jnp.zeros_like(key_sum_ref)
        value_sum_ref[...] = jnp.zeros_like(value_sum_ref)

    coefficient = coefficient_ref[...]
    mixed_grad = coefficient[:, 0:1] * score_out_ref[...] - coefficient[:, 1:2] * hidden_out_ref[...]
    mixed_grad = mixed_grad.astype(jnp.bfloat16)
    query = query_ref[...]
    value = value_ref[...]
    outs = []
    key_sum = key_sum_ref[...]
    value_sum = value_sum_ref[...]
    for head in range(HEADS_HERE):
        prob_grad = matmul(value * head_mask(head, jnp.bfloat16), mixed_grad, SUM_COLUMNS)
        prob_low = prob_ref[head]
        prob = prob_low.astype(jnp.float32)
        delta = jnp.sum(prob * prob_grad, axis=0, keepdims=True)
        score_grad = (prob * ((prob_grad - delta) * HD ** (-0.5))).astype(jnp.bfloat16)
        mask = head_mask(head, jnp.float32)
        key_sum = key_sum + matmul(score_grad, query) * mask
        value_sum = value_sum + matmul(prob_low, mixed_grad) * mask
        outs.append(matmul(flipped_ref[head * HD : (head + 1) * HD, :], score_grad))
    key_sum_ref[...] = key_sum
    value_sum_ref[...] = value_sum
    query_grad_ref[...] = jnp.concatenate(outs, axis=0).T.astype(jnp.bfloat16)

    @pl.when(step == pl.num_programs(0) - 1)
    def _():
        key_grad_ref[...] = key_sum_ref[...].astype(jnp.bfloat16)
        value_grad_ref[...] = value_sum_ref[...].astype(jnp.bfloat16)


def attend_grads(query, key, value, prob, hidden_out, coefficient, score_out):
    tokens, width = query.shape
    memory_rows = key.shape[0]
    whole = pl.BlockSpec((memory_rows, width), lambda i: (0, 0))
    block = pl.BlockSpec((TOKEN_BLOCK, width), lambda i: (i, 0))
    return pl.pallas_call(
        attend_grads_kernel,
        grid=(tokens // TOKEN_BLOCK,),
        in_specs=[
            block,
            whole,
            whole,
            pl.BlockSpec((HEADS_HERE, memory_rows, TOKEN_BLOCK), lambda i: (0, 0, i)),
            block,
            pl.BlockSpec((TOKEN_BLOCK, 2), lambda i: (i, 0)),
            pl.BlockSpec((1, width), lambda i: (0, 0)),
        ],
        out_specs=[block, whole, whole],
        out_shape=[
            jax.ShapeDtypeStruct((tokens, width), jnp.bfloat16),
            jax.ShapeDtypeStruct((memory_rows, width), jnp.bfloat16),
            jax.ShapeDtypeStruct((memory_rows, width), jnp.bfloat16),
        ],
        scratch_shapes=[
            pltpu.VMEM((width, memory_rows), jnp.bfloat16),
            pltpu.VMEM((memory_rows, width), jnp.float32),
            pltpu.VMEM((memory_rows, width), jnp.float32),
        ],
        compiler_params=pltpu.CompilerParams(vmem_limit_bytes=24 * 1024 * 1024),
        name="attend_grads",
    )(query, key, value, prob, hidden_out, coefficient, score_out)


def head_kernel(
    counts_ref,
    sums_ref,
    hidden_ref,
    weighted_ref,
    rank_ref,
    visits_ref,
    hidden_grad_ref,
    coefficient_ref,
    log_ref,
    loss_ref,
):
    tokens, slots = sums_ref.shape[0], rank_ref.shape[1]
    per_tactic = tokens // slots
    model_width = 4 * hidden_ref.shape[1]
    inverse = lax.rsqrt(sums_ref[:, 0:1] / model_width + 1e-06)
    raw = sums_ref[:, 1:2]
    token = lax.broadcasted_iota(jnp.int32, (tokens, slots), 0)
    first = lax.broadcasted_iota(jnp.int32, (tokens, slots), 1) * per_tactic
    member = (token >= first) & (token < first + per_tactic)
    logits = jnp.sum(jnp.where(member, inverse * raw, 0.0), axis=0, keepdims=True) / per_tactic
    live = rank_ref[...] < counts_ref[0]
    masked = jnp.where(live, logits, -1e30)
    top_value = jnp.max(masked, axis=1, keepdims=True)
    exponent = jnp.where(live, jnp.exp(masked - top_value), 0.0)
    log_total = top_value + jnp.log(jnp.sum(exponent, axis=1, keepdims=True))
    log_weight = jnp.where(live, logits - log_total, 0.0)
    visit_mass = jnp.where(live, visits_ref[...].astype(jnp.float32), 0.0)
    target = visit_mass / jnp.sum(visit_mass, axis=1, keepdims=True)
    log_ref[...] = log_weight
    loss_ref[...] = -jnp.sum(target * log_weight, axis=1, keepdims=True)
    logit_grad = jnp.where(live, jnp.exp(log_weight) - target, 0.0) / per_tactic
    tok_grad = jnp.sum(jnp.where(member, logit_grad, 0.0), axis=1, keepdims=True)
    near = inverse * tok_grad
    far = inverse * inverse * inverse * tok_grad * raw / model_width
    hidden_grad_ref[...] = (near * weighted_ref[...] - hidden_ref[...] * far).astype(jnp.bfloat16)
    coefficient_ref[:, 0:1] = near
    coefficient_ref[:, 1:2] = far


def policy_head(counts, sums, hidden, weighted, rank, visits):
    in_vmem = pl.BlockSpec(memory_space=pltpu.VMEM)
    tokens, width = hidden.shape
    slots = rank.shape[1]
    return pl.pallas_call(
        head_kernel,
        in_specs=[pl.BlockSpec(memory_space=pltpu.SMEM)] + [in_vmem] * 5,
        out_specs=[in_vmem] * 4,
        out_shape=[
            jax.ShapeDtypeStruct((tokens, width), jnp.bfloat16),
            jax.ShapeDtypeStruct((tokens, 2), jnp.float32),
            jax.ShapeDtypeStruct((1, slots), jnp.float32),
            jax.ShapeDtypeStruct((1, 1), jnp.float32),
        ],
        compiler_params=pltpu.CompilerParams(vmem_limit_bytes=16 * 1024 * 1024),
        name="policy_head",
    )(counts, sums, hidden, weighted, rank, visits)


def matmul(left, right, contract=(((1,), (0,)), ((), ()))):
    return lax.dot_general(left, right, contract, preferred_element_type=jnp.float32)


def body(dec_states, memory, counts, rank, visits, w_query, w_key, w_value, w_out, gain, w_score):
    model_width, width = w_query.shape
    slot_here, per_tactic = dec_states.shape[1:3]
    own_rows = slot_here * per_tactic
    slots = 16 * slot_here
    total_rows = slots * per_tactic
    slice_width = model_width // 4
    cand = lax.axis_index("cand")
    goal = lax.axis_index("goal")
    y = cand & 3
    core = goal & 1
    goal_bits = pair_bits(goal >> 1)

    own = jnp.concatenate([dec_states[0].reshape(own_rows, model_width), memory[0]], axis=0)
    parts = gather_cand(own, pair_bits(cand >> 2) + pair_bits(y))
    rows = jnp.concatenate(
        [part[..., :own_rows, :].reshape(total_rows, -1) for part in parts], axis=1
    )
    memory_all = jnp.concatenate(
        [part[..., own_rows:, :].reshape(16 * memory.shape[1], -1) for part in parts], axis=1
    )
    rows, memory_all, w_out = lax.optimization_barrier((rows, memory_all, w_out))
    w_slice = spread_out_weights(w_out, y, core)

    query = low(matmul(rows, w_query))
    key = low(matmul(memory_all, w_key))
    value = low(matmul(memory_all, w_value))
    mixed, prob = attend(query, key, value)

    weighted = gain * w_score
    score_out = jnp.sum(w_out.astype(jnp.float32) * weighted[None, :], axis=1)
    order = jnp.array([c * slot_here + s for c in cand_order() for s in range(slot_here)], jnp.int32)
    pick = order[None, :] == jnp.arange(slots, dtype=jnp.int32)[:, None]
    rank_here = jnp.sum(jnp.where(pick, rank[0][:, None], 0), axis=0, keepdims=True)
    visits_here = jnp.sum(jnp.where(pick, visits[0][:, None], 0), axis=0, keepdims=True)

    mixed_line = gather_heads(mixed)
    attended = sum_line(matmul(mixed_line, w_slice))
    hidden = lax.dynamic_slice_in_dim(rows, y * slice_width, slice_width, 1).astype(jnp.float32)
    hidden = hidden + attended
    weighted_slice = lax.dynamic_slice_in_dim(weighted, y * slice_width, slice_width, 0)
    sums = jnp.stack([jnp.sum(hidden * hidden, axis=1), jnp.sum(hidden * weighted_slice, axis=1)])
    sums = sums + swap_cand(sums, Y_MASKS[0])
    kept = scatter_heads_start(matmul(low(hidden), w_slice, SUM_COLUMNS), width)
    sums = sums + swap_cand(sums, Y_MASKS[1])
    kept, sums = lax.optimization_barrier((kept, sums))
    hidden_out = scatter_heads_end(kept, width)
    hidden_grad, coefficient, log_weight, loss = policy_head(
        counts, sums.T, hidden, weighted_slice[None, :], rank_here, visits_here
    )

    keep, send = core_halves(hidden_grad, core)
    hidden_grad_both = jnp.concatenate([keep, swap_goal(send, 1)], axis=0)
    out_lines = low(matmul(both_cores(mixed_line), hidden_grad_both, SUM_ROWS))
    grad_out = sum_z(out_lines.reshape(1, 4, width, -1), goal_bits)[0]
    pairs = []
    for g in range(8):
        for c in range(16):
            goal_to = 2 * (c & 3) + (g & 1)
            pairs.append((16 * g + c, 16 * goal_to + (c ^ (g >> 1))))
    grad_out = lax.ppermute(grad_out, ("goal", "cand"), pairs)

    query_grad, key_grad, value_grad = attend_grads(
        query, key, value, prob, hidden_out, coefficient, score_out[None, :]
    )
    rows_both = share_columns(rows, core)
    memory_both = share_columns(memory_all, core)
    value_lines = low(matmul(memory_both, both_cores(value_grad), SUM_ROWS))
    grad_value = sum_z(value_lines.reshape(1, 4, -1, width), goal_bits)[0]
    key_lines = low(matmul(memory_both, both_cores(key_grad), SUM_ROWS))
    query_lines = low(matmul(rows_both, both_cores(query_grad), SUM_ROWS))
    both_lines = jnp.concatenate([query_lines, key_lines]).reshape(2, 4, -1, width)
    grad_both = sum_z(both_lines, goal_bits)
    own_slots = cand * slot_here + jnp.arange(slot_here, dtype=jnp.int32)
    own_log = jnp.sum(
        jnp.where(own_slots[:, None] == order[None, :], log_weight, 0.0), axis=1
    )
    return own_log[None, :], loss[0], grad_both[0], grad_both[1], grad_value, grad_out


def solution(mesh):
    return jax.shard_map(
        body,
        mesh=mesh,
        in_specs=(
            P("goal", "cand", None, None),
            P("goal", "cand", None),
            P("goal"),
            P("goal", None),
            P("goal", None),
            P(None, "cand"),
            P(None, "cand"),
            P(None, "cand"),
            P("cand", None),
            P(),
            P(),
        ),
        out_specs=(
            P("goal", "cand"),
            P("goal"),
            P("goal", "cand"),
            P("goal", "cand"),
            P("goal", "cand"),
            P("cand", "goal"),
        ),
        check_vma=False,
    )
```

```python
import jax
import jax.numpy as jnp
from jax import lax
from jax.experimental import pallas as pl
from jax.experimental.pallas import tpu as pltpu
from jax.sharding import PartitionSpec as P

HD = 64
HEADS_HERE = 4
TOKEN_BLOCK = 256
X_MASKS = (4, 12)
Y_MASKS = (1, 3)
CAND_MASKS = X_MASKS + Y_MASKS
GOAL_MASKS = (2, 6)
PART_ORDERS = ((0, 1, 2, 3), (1, 0, 3, 2), (2, 3, 0, 1), (3, 2, 1, 0))
SUM_ROWS = (((0,), (0,)), ((), ()))
SUM_COLUMNS = (((1,), (1,)), ((), ()))


def swap_cand(values, mask):
    return lax.ppermute(values, "cand", [(i, i ^ mask) for i in range(16)])


def swap_goal(values, mask):
    return lax.ppermute(values, "goal", [(i, i ^ mask) for i in range(8)])


def exchange(parts, masks, swap=swap_cand):
    parts = lax.optimization_barrier(list(parts))
    return lax.optimization_barrier([swap(part, mask) for part, mask in zip(parts, masks)])


def plus(left, right):
    return left.astype(jnp.float32) + right.astype(jnp.float32)


def low(values):
    return values.astype(jnp.bfloat16)


def pair_bits(coordinate):
    high = coordinate >> 1
    return ((coordinate & 1) ^ high, high)


def cand_order():
    order = []
    for position in range(16):
        bits = [(position >> i) & 1 for i in range(4)]
        order.append(4 * (bits[0] ^ (3 * bits[1])) + (bits[2] ^ (3 * bits[3])))
    return order


def gather_cand(own, bits, early):
    parts = [part[None, None, None, None] for part in jnp.split(own, 4, axis=1)]
    for step in range(4):
        masks = [CAND_MASKS[order[step]] for order in PART_ORDERS]
        if step < 2:
            others = exchange(parts, masks)
        else:
            if step == 2:
                parts, early = lax.optimization_barrier((parts, early))
            others = [swap_cand(part, mask) for part, mask in zip(parts, masks)]
            if step == 3:
                others, early = lax.optimization_barrier((others, early))
        merged = []
        for part, other, order in zip(parts, others, PART_ORDERS):
            bit = bits[order[step]]
            first = jnp.where(bit == 0, part, other)
            second = jnp.where(bit == 0, other, part)
            merged.append(jnp.concatenate([first, second], axis=3 - order[step]))
        parts = merged
    return parts, early


def cut_out_weights(w_out, y, core):
    height, width = w_out.shape[0] // 2, w_out.shape[1] // 4
    return [
        lax.dynamic_slice(w_out, (core * height, (y ^ mask) * width), (height, width))
        for mask in (1, 3, 2)
    ]


def fetch_out_weights(cut):
    got = jnp.concatenate(exchange(cut, (1, 3, 2)), axis=0)
    return got, swap_goal(got, 1)


def join_out_weights(w_out, got, other, y, core):
    height, width = got.shape[0] // 3, got.shape[1]
    first = jnp.where(core == 0, got, other).reshape(3, height, width)
    second = jnp.where(core == 0, other, got).reshape(3, height, width)
    received = jnp.stack([first, second], axis=1).reshape(6 * height, width)
    own = lax.dynamic_slice_in_dim(w_out, y * width, width, 1)
    return jnp.concatenate([own, received], axis=0)


def gather_heads(mixed, fetched):
    halves = jnp.split(mixed, 2, axis=0)
    near = exchange(halves, Y_MASKS)
    pairs = [jnp.concatenate([half, other], axis=1) for half, other in zip(halves, near)]
    pairs, fetched = lax.optimization_barrier((pairs, fetched))
    far = exchange(pairs, Y_MASKS[::-1])
    width = mixed.shape[1]
    second = jnp.concatenate(
        [halves[1], far[1][:, :width], near[1], far[1][:, width:]], axis=1
    )
    first = jnp.concatenate([halves[0], near[0], far[0]], axis=1)
    return jnp.concatenate([first, second], axis=0), fetched


def sum_line(values):
    parts = jnp.split(low(values), 2, axis=1)
    for masks in (X_MASKS, X_MASKS[::-1]):
        others = exchange(parts, masks)
        totals = [plus(part, other) for part, other in zip(parts, others)]
        parts = [low(total) for total in totals]
    return jnp.concatenate(totals, axis=1)


def scatter_heads_start(values, sums, width):
    halves = jnp.split(values, 2, axis=0)
    blocks = [[half[:, i * width : (i + 1) * width] for i in range(4)] for half in halves]
    keep = [jnp.concatenate(blocks[0][:2], axis=1), jnp.concatenate(blocks[1][::2], axis=1)]
    send = [jnp.concatenate(blocks[0][2:], axis=1), jnp.concatenate(blocks[1][1::2], axis=1)]
    others = exchange(send + [sums] * 3, Y_MASKS[::-1] + (1, 3, 2))
    kept = [low(plus(part, other)) for part, other in zip(keep, others)]
    return kept, (sums + others[2]) + (others[3] + others[4])


def scatter_heads_end(kept, width):
    others = exchange([part[:, width:] for part in kept], Y_MASKS)
    return jnp.concatenate(
        [plus(part[:, :width], other) for part, other in zip(kept, others)], axis=0
    )


def core_halves(values, core):
    half = values.shape[1] // 2
    left, right = values[:, :half], values[:, half:]
    return jnp.where(core == 0, left, right), jnp.where(core == 0, right, left)


def both_cores(values):
    return jnp.concatenate([values, swap_goal(values, 1)], axis=0)


def share_columns(values, core):
    quarters = [core_halves(part, core) for part in jnp.split(values, 4, axis=1)]
    quarters = [quarters[i] for i in (0, 1, 3, 2)]
    keep = jnp.concatenate([quarter[0] for quarter in quarters], axis=1)
    send = jnp.concatenate([quarter[1] for quarter in quarters], axis=1)
    return jnp.concatenate([keep, swap_goal(send, 1)], axis=0)


def sum_z_step(zeros, ones, bits, turn):
    which = (turn, 1 - turn)
    sends = [jnp.where(bits[w] == 0, one, zero) for w, zero, one in zip(which, zeros, ones)]
    keeps = [jnp.where(bits[w] == 0, zero, one) for w, zero, one in zip(which, zeros, ones)]
    others = exchange(sends, [GOAL_MASKS[w] for w in which], swap_goal)
    return [low(plus(part, other)) for part, other in zip(keeps, others)]


def sum_z_start(lines, bits):
    count, _, height, width = lines.shape
    lines = lines.reshape(count, 2, 2, height, width)
    parts = [lines[:, :, :, : height // 2], lines[:, :, :, height // 2 :]]
    zeros = [parts[0][:, :, 0], parts[1][:, 0]]
    ones = [parts[0][:, :, 1], parts[1][:, 1]]
    return sum_z_step(zeros, ones, bits, 0)


def sum_z_end(sums, bits):
    sums = sum_z_step([part[:, 0] for part in sums], [part[:, 1] for part in sums], bits, 1)
    return jnp.concatenate(sums, axis=1)


def sum_z(lines, bits):
    return sum_z_end(sum_z_start(lines, bits), bits)


def head_mask(head, dtype):
    lane = lax.broadcasted_iota(jnp.int32, (1, HEADS_HERE * HD), 1)
    inside = (lane >= head * HD) & (lane < (head + 1) * HD)
    return jnp.where(inside, 1.0, 0.0).astype(dtype)


def attend_kernel(query_ref, key_ref, value_ref, mixed_ref, prob_ref, flipped_ref):
    @pl.when(pl.program_id(0) == 0)
    def _():
        flipped_ref[...] = value_ref[...].astype(jnp.float32).T.astype(jnp.bfloat16)

    query = query_ref[...] * jnp.bfloat16(HD ** (-0.5))
    key = key_ref[...]
    outs = []
    for head in range(HEADS_HERE):
        scores = matmul(key * head_mask(head, jnp.bfloat16), query, SUM_COLUMNS)
        exponent = jnp.exp(scores - jnp.max(scores, axis=0, keepdims=True))
        share = 1.0 / jnp.sum(exponent, axis=0, keepdims=True)
        prob = (exponent * share).astype(jnp.bfloat16)
        prob_ref[head] = prob
        outs.append(matmul(flipped_ref[head * HD : (head + 1) * HD, :], prob))
    mixed_ref[...] = jnp.concatenate(outs, axis=0).T.astype(jnp.bfloat16)


def attend(query, key, value):
    tokens, width = query.shape
    memory_rows = key.shape[0]
    whole = pl.BlockSpec((memory_rows, width), lambda i: (0, 0))
    block = pl.BlockSpec((TOKEN_BLOCK, width), lambda i: (i, 0))
    return pl.pallas_call(
        attend_kernel,
        grid=(tokens // TOKEN_BLOCK,),
        in_specs=[block, whole, whole],
        out_specs=[
            block,
            pl.BlockSpec((HEADS_HERE, memory_rows, TOKEN_BLOCK), lambda i: (0, 0, i)),
        ],
        out_shape=[
            jax.ShapeDtypeStruct((tokens, width), jnp.bfloat16),
            jax.ShapeDtypeStruct((HEADS_HERE, memory_rows, tokens), jnp.bfloat16),
        ],
        scratch_shapes=[pltpu.VMEM((width, memory_rows), jnp.bfloat16)],
        compiler_params=pltpu.CompilerParams(vmem_limit_bytes=24 * 1024 * 1024),
        name="attend",
    )(query, key, value)


def attend_grads_kernel(
    query_ref,
    key_ref,
    value_ref,
    prob_ref,
    hidden_out_ref,
    coefficient_ref,
    score_out_ref,
    query_grad_ref,
    key_grad_ref,
    value_grad_ref,
    flipped_ref,
    key_sum_ref,
    value_sum_ref,
):
    step = pl.program_id(0)

    @pl.when(step == 0)
    def _():
        flipped_ref[...] = key_ref[...].astype(jnp.float32).T.astype(jnp.bfloat16)
        key_sum_ref[...] = jnp.zeros_like(key_sum_ref)
        value_sum_ref[...] = jnp.zeros_like(value_sum_ref)

    coefficient = coefficient_ref[...]
    mixed_grad = coefficient[:, 0:1] * score_out_ref[...] - coefficient[:, 1:2] * hidden_out_ref[...]
    mixed_grad = mixed_grad.astype(jnp.bfloat16)
    query = query_ref[...]
    value = value_ref[...]
    outs = []
    key_sum = key_sum_ref[...]
    value_sum = value_sum_ref[...]
    for head in range(HEADS_HERE):
        prob_grad = matmul(value * head_mask(head, jnp.bfloat16), mixed_grad, SUM_COLUMNS)
        prob_low = prob_ref[head]
        prob = prob_low.astype(jnp.float32)
        delta = jnp.sum(prob * prob_grad, axis=0, keepdims=True)
        score_grad = (prob * ((prob_grad - delta) * HD ** (-0.5))).astype(jnp.bfloat16)
        mask = head_mask(head, jnp.float32)
        key_sum = key_sum + matmul(score_grad, query) * mask
        value_sum = value_sum + matmul(prob_low, mixed_grad) * mask
        outs.append(matmul(flipped_ref[head * HD : (head + 1) * HD, :], score_grad))
    key_sum_ref[...] = key_sum
    value_sum_ref[...] = value_sum
    query_grad_ref[...] = jnp.concatenate(outs, axis=0).T.astype(jnp.bfloat16)

    @pl.when(step == pl.num_programs(0) - 1)
    def _():
        key_grad_ref[...] = key_sum_ref[...].astype(jnp.bfloat16)
        value_grad_ref[...] = value_sum_ref[...].astype(jnp.bfloat16)


def attend_grads(query, key, value, prob, hidden_out, coefficient, score_out):
    tokens, width = query.shape
    memory_rows = key.shape[0]
    whole = pl.BlockSpec((memory_rows, width), lambda i: (0, 0))
    block = pl.BlockSpec((TOKEN_BLOCK, width), lambda i: (i, 0))
    return pl.pallas_call(
        attend_grads_kernel,
        grid=(tokens // TOKEN_BLOCK,),
        in_specs=[
            block,
            whole,
            whole,
            pl.BlockSpec((HEADS_HERE, memory_rows, TOKEN_BLOCK), lambda i: (0, 0, i)),
            block,
            pl.BlockSpec((TOKEN_BLOCK, 2), lambda i: (i, 0)),
            pl.BlockSpec((1, width), lambda i: (0, 0)),
        ],
        out_specs=[block, whole, whole],
        out_shape=[
            jax.ShapeDtypeStruct((tokens, width), jnp.bfloat16),
            jax.ShapeDtypeStruct((memory_rows, width), jnp.bfloat16),
            jax.ShapeDtypeStruct((memory_rows, width), jnp.bfloat16),
        ],
        scratch_shapes=[
            pltpu.VMEM((width, memory_rows), jnp.bfloat16),
            pltpu.VMEM((memory_rows, width), jnp.float32),
            pltpu.VMEM((memory_rows, width), jnp.float32),
        ],
        compiler_params=pltpu.CompilerParams(vmem_limit_bytes=24 * 1024 * 1024),
        name="attend_grads",
    )(query, key, value, prob, hidden_out, coefficient, score_out)


def head_kernel(
    counts_ref,
    sums_ref,
    hidden_ref,
    weighted_ref,
    rank_ref,
    visits_ref,
    hidden_grad_ref,
    coefficient_ref,
    log_ref,
    loss_ref,
):
    tokens, slots = sums_ref.shape[1], rank_ref.shape[1]
    per_tactic = tokens // slots
    model_width = 4 * hidden_ref.shape[1]
    sums = jnp.concatenate([sums_ref[...], jnp.zeros((6, tokens), jnp.float32)], axis=0).T
    inverse = lax.rsqrt(sums[:, 0:1] / model_width + 1e-06)
    raw = sums[:, 1:2]
    token = lax.broadcasted_iota(jnp.int32, (tokens, slots), 0)
    first = lax.broadcasted_iota(jnp.int32, (tokens, slots), 1) * per_tactic
    member = (token >= first) & (token < first + per_tactic)
    logits = jnp.sum(jnp.where(member, inverse * raw, 0.0), axis=0, keepdims=True) / per_tactic
    live = rank_ref[...] < counts_ref[0]
    masked = jnp.where(live, logits, -1e30)
    top_value = jnp.max(masked, axis=1, keepdims=True)
    exponent = jnp.where(live, jnp.exp(masked - top_value), 0.0)
    log_total = top_value + jnp.log(jnp.sum(exponent, axis=1, keepdims=True))
    log_weight = jnp.where(live, logits - log_total, 0.0)
    visit_mass = jnp.where(live, visits_ref[...].astype(jnp.float32), 0.0)
    target = visit_mass / jnp.sum(visit_mass, axis=1, keepdims=True)
    log_ref[...] = log_weight
    loss_ref[...] = -jnp.sum(target * log_weight, axis=1, keepdims=True)
    logit_grad = jnp.where(live, jnp.exp(log_weight) - target, 0.0) / per_tactic
    tok_grad = jnp.sum(jnp.where(member, logit_grad, 0.0), axis=1, keepdims=True)
    near = inverse * tok_grad
    far = inverse * inverse * inverse * tok_grad * raw / model_width
    hidden_grad_ref[...] = (near * weighted_ref[...] - hidden_ref[...] * far).astype(jnp.bfloat16)
    coefficient_ref[:, 0:1] = near
    coefficient_ref[:, 1:2] = far


def policy_head(counts, sums, hidden, weighted, rank, visits):
    in_vmem = pl.BlockSpec(memory_space=pltpu.VMEM)
    tokens, width = hidden.shape
    slots = rank.shape[1]
    return pl.pallas_call(
        head_kernel,
        in_specs=[pl.BlockSpec(memory_space=pltpu.SMEM)] + [in_vmem] * 5,
        out_specs=[in_vmem] * 4,
        out_shape=[
            jax.ShapeDtypeStruct((tokens, width), jnp.bfloat16),
            jax.ShapeDtypeStruct((tokens, 2), jnp.float32),
            jax.ShapeDtypeStruct((1, slots), jnp.float32),
            jax.ShapeDtypeStruct((1, 1), jnp.float32),
        ],
        compiler_params=pltpu.CompilerParams(vmem_limit_bytes=16 * 1024 * 1024),
        name="policy_head",
    )(counts, sums, hidden, weighted, rank, visits)


def matmul(left, right, contract=(((1,), (0,)), ((), ()))):
    return lax.dot_general(left, right, contract, preferred_element_type=jnp.float32)


def body(dec_states, memory, counts, rank, visits, w_query, w_key, w_value, w_out, gain, w_score):
    model_width, width = w_query.shape
    slot_here, per_tactic = dec_states.shape[1:3]
    own_rows = slot_here * per_tactic
    slots = 16 * slot_here
    total_rows = slots * per_tactic
    slice_width = model_width // 4
    cand = lax.axis_index("cand")
    goal = lax.axis_index("goal")
    y = cand & 3
    core = goal & 1
    goal_bits = pair_bits(goal >> 1)

    own = jnp.concatenate([dec_states[0].reshape(own_rows, model_width), memory[0]], axis=0)
    bits = pair_bits(cand >> 2) + pair_bits(y)
    parts, cut = gather_cand(own, bits, cut_out_weights(w_out, y, core))
    rows = jnp.concatenate(
        [part[..., :own_rows, :].reshape(total_rows, -1) for part in parts], axis=1
    )
    memory_all = jnp.concatenate(
        [part[..., own_rows:, :].reshape(16 * memory.shape[1], -1) for part in parts], axis=1
    )
    fetched = fetch_out_weights(cut)

    query = low(matmul(rows, w_query))
    key = low(matmul(memory_all, w_key))
    value = low(matmul(memory_all, w_value))
    mixed, prob = attend(query, key, value)

    weighted = gain * w_score
    score_out = jnp.sum(w_out.astype(jnp.float32) * weighted[None, :], axis=1)
    order = jnp.array([c * slot_here + s for c in cand_order() for s in range(slot_here)], jnp.int32)
    pick = order[None, :] == jnp.arange(slots, dtype=jnp.int32)[:, None]
    rank_here = jnp.sum(jnp.where(pick, rank[0][:, None], 0), axis=0, keepdims=True)
    visits_here = jnp.sum(jnp.where(pick, visits[0][:, None], 0), axis=0, keepdims=True)

    mixed_line, (got, other) = gather_heads(mixed, fetched)
    w_slice = join_out_weights(w_out, got, other, y, core)
    attended = sum_line(matmul(mixed_line, w_slice))
    hidden = lax.dynamic_slice_in_dim(rows, y * slice_width, slice_width, 1).astype(jnp.float32)
    hidden = hidden + attended
    weighted_slice = lax.dynamic_slice_in_dim(weighted, y * slice_width, slice_width, 0)
    sums = jnp.stack([jnp.sum(hidden * hidden, axis=1), jnp.sum(hidden * weighted_slice, axis=1)])
    kept, sums = scatter_heads_start(low(matmul(low(hidden), w_slice, SUM_COLUMNS)), sums, width)
    hidden_out = scatter_heads_end(kept, width)
    hidden_grad, coefficient, log_weight, loss = policy_head(
        counts, sums, hidden, weighted_slice[None, :], rank_here, visits_here
    )

    keep, send = core_halves(hidden_grad, core)
    hidden_grad_both = jnp.concatenate([keep, swap_goal(send, 1)], axis=0)
    out_lines = low(matmul(both_cores(mixed_line), hidden_grad_both, SUM_ROWS))
    hidden_out, out_lines = lax.optimization_barrier((hidden_out, out_lines))
    grad_out = sum_z(out_lines.reshape(1, 4, width, -1), goal_bits)[0]
    pairs = []
    for g in range(8):
        for c in range(16):
            goal_to = 2 * (c & 3) + (g & 1)
            pairs.append((16 * g + c, 16 * goal_to + (c ^ (g >> 1))))
    grad_out = lax.ppermute(grad_out, ("goal", "cand"), pairs)

    query_grad, key_grad, value_grad = attend_grads(
        query, key, value, prob, hidden_out, coefficient, score_out[None, :]
    )
    rows_both = share_columns(rows, core)
    memory_both = share_columns(memory_all, core)
    value_lines = low(matmul(memory_both, both_cores(value_grad), SUM_ROWS))
    grad_value = sum_z(value_lines.reshape(1, 4, -1, width), goal_bits)[0]
    key_lines = low(matmul(memory_both, both_cores(key_grad), SUM_ROWS))
    query_lines = low(matmul(rows_both, both_cores(query_grad), SUM_ROWS))
    both_lines = jnp.concatenate([query_lines, key_lines]).reshape(2, 4, -1, width)
    grad_both = sum_z(both_lines, goal_bits)
    own_slots = cand * slot_here + jnp.arange(slot_here, dtype=jnp.int32)
    own_log = jnp.sum(
        jnp.where(own_slots[:, None] == order[None, :], log_weight, 0.0), axis=1
    )
    return own_log[None, :], loss[0], grad_both[0], grad_both[1], grad_value, grad_out


def solution(mesh):
    return jax.shard_map(
        body,
        mesh=mesh,
        in_specs=(
            P("goal", "cand", None, None),
            P("goal", "cand", None),
            P("goal"),
            P("goal", None),
            P("goal", None),
            P(None, "cand"),
            P(None, "cand"),
            P(None, "cand"),
            P("cand", None),
            P(),
            P(),
        ),
        out_specs=(
            P("goal", "cand"),
            P("goal"),
            P("goal", "cand"),
            P("goal", "cand"),
            P("goal", "cand"),
            P("cand", "goal"),
        ),
        check_vma=False,
    )
```

```python
import jax
import jax.numpy as jnp
from jax import lax
from jax.experimental import pallas as pl
from jax.experimental.pallas import tpu as pltpu
from jax.sharding import PartitionSpec as P

HD = 64
HEADS_HERE = 4
TOKEN_BLOCK = 256
X_MASKS = (4, 12)
Y_MASKS = (1, 3)
CAND_MASKS = X_MASKS + Y_MASKS
GOAL_MASKS = (2, 6)
PART_ORDERS = ((0, 1, 2, 3), (1, 0, 3, 2), (2, 3, 0, 1), (3, 2, 1, 0))
SUM_ROWS = (((0,), (0,)), ((), ()))
SUM_COLUMNS = (((1,), (1,)), ((), ()))


def swap_cand(values, mask):
    return lax.ppermute(values, "cand", [(i, i ^ mask) for i in range(16)])


def swap_goal(values, mask):
    return lax.ppermute(values, "goal", [(i, i ^ mask) for i in range(8)])


def exchange(parts, masks, swap=swap_cand):
    parts = lax.optimization_barrier(list(parts))
    return lax.optimization_barrier([swap(part, mask) for part, mask in zip(parts, masks)])


def plus(left, right):
    return left.astype(jnp.float32) + right.astype(jnp.float32)


def low(values):
    return values.astype(jnp.bfloat16)


def pair_bits(coordinate):
    high = coordinate >> 1
    return ((coordinate & 1) ^ high, high)


def cand_order():
    order = []
    for position in range(16):
        bits = [(position >> i) & 1 for i in range(4)]
        order.append(4 * (bits[0] ^ (3 * bits[1])) + (bits[2] ^ (3 * bits[3])))
    return order


def gather_cand(own, bits, early):
    parts = [part[None, None, None, None] for part in jnp.split(own, 4, axis=1)]
    for step in range(4):
        masks = [CAND_MASKS[order[step]] for order in PART_ORDERS]
        if step < 2:
            others = exchange(parts, masks)
        else:
            if step == 3:
                parts, early = lax.optimization_barrier((parts, early))
            others = [swap_cand(part, mask) for part, mask in zip(parts, masks)]
            if step == 3:
                others, early = lax.optimization_barrier((others, early))
        merged = []
        for part, other, order in zip(parts, others, PART_ORDERS):
            bit = bits[order[step]]
            first = jnp.where(bit == 0, part, other)
            second = jnp.where(bit == 0, other, part)
            merged.append(jnp.concatenate([first, second], axis=3 - order[step]))
        parts = merged
    return parts, early


def cut_out_weights(w_out, y, core):
    height, width = w_out.shape[0] // 2, w_out.shape[1] // 4
    return [
        lax.dynamic_slice(w_out, (core * height, (y ^ mask) * width), (height, width))
        for mask in (1, 3, 2)
    ]


def fetch_out_weights(cut):
    got = jnp.concatenate(exchange(cut, (1, 3, 2)), axis=0)
    return got, swap_goal(got, 1)


def join_out_weights(w_out, got, other, y, core):
    height, width = got.shape[0] // 3, got.shape[1]
    first = jnp.where(core == 0, got, other).reshape(3, height, width)
    second = jnp.where(core == 0, other, got).reshape(3, height, width)
    received = jnp.stack([first, second], axis=1).reshape(6 * height, width)
    own = lax.dynamic_slice_in_dim(w_out, y * width, width, 1)
    return jnp.concatenate([own, received], axis=0)


def gather_heads(mixed, fetched):
    halves = jnp.split(mixed, 2, axis=0)
    near = exchange(halves, Y_MASKS)
    pairs = [jnp.concatenate([half, other], axis=1) for half, other in zip(halves, near)]
    pairs, fetched = lax.optimization_barrier((pairs, fetched))
    far = exchange(pairs, Y_MASKS[::-1])
    width = mixed.shape[1]
    second = jnp.concatenate(
        [halves[1], far[1][:, :width], near[1], far[1][:, width:]], axis=1
    )
    first = jnp.concatenate([halves[0], near[0], far[0]], axis=1)
    return jnp.concatenate([first, second], axis=0), fetched


def sum_line(values):
    parts = jnp.split(low(values), 2, axis=1)
    for masks in (X_MASKS, X_MASKS[::-1]):
        others = exchange(parts, masks)
        totals = [plus(part, other) for part, other in zip(parts, others)]
        parts = [low(total) for total in totals]
    return jnp.concatenate(totals, axis=1)


def scatter_heads_start(values, sums, width):
    halves = jnp.split(values, 2, axis=0)
    blocks = [[half[:, i * width : (i + 1) * width] for i in range(4)] for half in halves]
    keep = [jnp.concatenate(blocks[0][:2], axis=1), jnp.concatenate(blocks[1][::2], axis=1)]
    send = [jnp.concatenate(blocks[0][2:], axis=1), jnp.concatenate(blocks[1][1::2], axis=1)]
    others = exchange(send + [sums] * 3, Y_MASKS[::-1] + (1, 3, 2))
    kept = [low(plus(part, other)) for part, other in zip(keep, others)]
    return kept, (sums + others[2]) + (others[3] + others[4])


def scatter_heads_end(kept, width):
    others = exchange([part[:, width:] for part in kept], Y_MASKS)
    return jnp.concatenate(
        [plus(part[:, :width], other) for part, other in zip(kept, others)], axis=0
    )


def core_halves(values, core):
    half = values.shape[1] // 2
    left, right = values[:, :half], values[:, half:]
    return jnp.where(core == 0, left, right), jnp.where(core == 0, right, left)


def share_columns(values, core):
    quarters = [core_halves(part, core) for part in jnp.split(values, 4, axis=1)]
    quarters = [quarters[i] for i in (0, 1, 3, 2)]
    keep = jnp.concatenate([quarter[0] for quarter in quarters], axis=1)
    send = jnp.concatenate([quarter[1] for quarter in quarters], axis=1)
    return keep, swap_goal(send, 1)


def both_terms(values, grads):
    return low(
        matmul(values[0], grads, SUM_ROWS) + matmul(values[1], swap_goal(grads, 1), SUM_ROWS)
    )


def sum_z_step(zeros, ones, bits, turn):
    which = (turn, 1 - turn)
    sends = [jnp.where(bits[w] == 0, one, zero) for w, zero, one in zip(which, zeros, ones)]
    keeps = [jnp.where(bits[w] == 0, zero, one) for w, zero, one in zip(which, zeros, ones)]
    others = exchange(sends, [GOAL_MASKS[w] for w in which], swap_goal)
    return [low(plus(part, other)) for part, other in zip(keeps, others)]


def sum_z_start(lines, bits):
    count, _, height, width = lines.shape
    lines = lines.reshape(count, 2, 2, height, width)
    parts = [lines[:, :, :, : height // 2], lines[:, :, :, height // 2 :]]
    zeros = [parts[0][:, :, 0], parts[1][:, 0]]
    ones = [parts[0][:, :, 1], parts[1][:, 1]]
    return sum_z_step(zeros, ones, bits, 0)


def sum_z_end(sums, bits):
    sums = sum_z_step([part[:, 0] for part in sums], [part[:, 1] for part in sums], bits, 1)
    return jnp.concatenate(sums, axis=1)


def sum_z(lines, bits):
    return sum_z_end(sum_z_start(lines, bits), bits)


def head_mask(head, dtype):
    lane = lax.broadcasted_iota(jnp.int32, (1, HEADS_HERE * HD), 1)
    inside = (lane >= head * HD) & (lane < (head + 1) * HD)
    return jnp.where(inside, 1.0, 0.0).astype(dtype)


def attend_kernel(query_ref, key_ref, value_ref, mixed_ref, prob_ref, flipped_ref):
    @pl.when(pl.program_id(0) == 0)
    def _():
        flipped_ref[...] = value_ref[...].astype(jnp.float32).T.astype(jnp.bfloat16)

    query = query_ref[...] * jnp.bfloat16(HD ** (-0.5))
    key = key_ref[...]
    outs = []
    for head in range(HEADS_HERE):
        scores = matmul(key * head_mask(head, jnp.bfloat16), query, SUM_COLUMNS)
        exponent = jnp.exp(scores - jnp.max(scores, axis=0, keepdims=True))
        share = 1.0 / jnp.sum(exponent, axis=0, keepdims=True)
        prob = (exponent * share).astype(jnp.bfloat16)
        prob_ref[head] = prob
        outs.append(matmul(flipped_ref[head * HD : (head + 1) * HD, :], prob))
    mixed_ref[...] = jnp.concatenate(outs, axis=0).T.astype(jnp.bfloat16)


def attend(query, key, value):
    tokens, width = query.shape
    memory_rows = key.shape[0]
    whole = pl.BlockSpec((memory_rows, width), lambda i: (0, 0))
    block = pl.BlockSpec((TOKEN_BLOCK, width), lambda i: (i, 0))
    return pl.pallas_call(
        attend_kernel,
        grid=(tokens // TOKEN_BLOCK,),
        in_specs=[block, whole, whole],
        out_specs=[
            block,
            pl.BlockSpec((HEADS_HERE, memory_rows, TOKEN_BLOCK), lambda i: (0, 0, i)),
        ],
        out_shape=[
            jax.ShapeDtypeStruct((tokens, width), jnp.bfloat16),
            jax.ShapeDtypeStruct((HEADS_HERE, memory_rows, tokens), jnp.bfloat16),
        ],
        scratch_shapes=[pltpu.VMEM((width, memory_rows), jnp.bfloat16)],
        compiler_params=pltpu.CompilerParams(vmem_limit_bytes=24 * 1024 * 1024),
        name="attend",
    )(query, key, value)


def attend_grads_kernel(
    query_ref,
    key_ref,
    value_ref,
    prob_ref,
    hidden_out_ref,
    coefficient_ref,
    score_out_ref,
    query_grad_ref,
    key_grad_ref,
    value_grad_ref,
    flipped_ref,
    key_sum_ref,
    value_sum_ref,
):
    step = pl.program_id(0)

    @pl.when(step == 0)
    def _():
        flipped_ref[...] = key_ref[...].astype(jnp.float32).T.astype(jnp.bfloat16)
        key_sum_ref[...] = jnp.zeros_like(key_sum_ref)
        value_sum_ref[...] = jnp.zeros_like(value_sum_ref)

    coefficient = coefficient_ref[...]
    mixed_grad = coefficient[:, 0:1] * score_out_ref[...] - coefficient[:, 1:2] * hidden_out_ref[...]
    mixed_grad = mixed_grad.astype(jnp.bfloat16)
    query = query_ref[...]
    value = value_ref[...]
    outs = []
    key_sum = key_sum_ref[...]
    value_sum = value_sum_ref[...]
    for head in range(HEADS_HERE):
        prob_grad = matmul(value * head_mask(head, jnp.bfloat16), mixed_grad, SUM_COLUMNS)
        prob_low = prob_ref[head]
        prob = prob_low.astype(jnp.float32)
        delta = jnp.sum(prob * prob_grad, axis=0, keepdims=True)
        score_grad = (prob * ((prob_grad - delta) * HD ** (-0.5))).astype(jnp.bfloat16)
        mask = head_mask(head, jnp.float32)
        key_sum = key_sum + matmul(score_grad, query) * mask
        value_sum = value_sum + matmul(prob_low, mixed_grad) * mask
        outs.append(matmul(flipped_ref[head * HD : (head + 1) * HD, :], score_grad))
    key_sum_ref[...] = key_sum
    value_sum_ref[...] = value_sum
    query_grad_ref[...] = jnp.concatenate(outs, axis=0).T.astype(jnp.bfloat16)

    @pl.when(step == pl.num_programs(0) - 1)
    def _():
        key_grad_ref[...] = key_sum_ref[...].astype(jnp.bfloat16)
        value_grad_ref[...] = value_sum_ref[...].astype(jnp.bfloat16)


def attend_grads(query, key, value, prob, hidden_out, coefficient, score_out):
    tokens, width = query.shape
    memory_rows = key.shape[0]
    whole = pl.BlockSpec((memory_rows, width), lambda i: (0, 0))
    block = pl.BlockSpec((TOKEN_BLOCK, width), lambda i: (i, 0))
    return pl.pallas_call(
        attend_grads_kernel,
        grid=(tokens // TOKEN_BLOCK,),
        in_specs=[
            block,
            whole,
            whole,
            pl.BlockSpec((HEADS_HERE, memory_rows, TOKEN_BLOCK), lambda i: (0, 0, i)),
            block,
            pl.BlockSpec((TOKEN_BLOCK, 2), lambda i: (i, 0)),
            pl.BlockSpec((1, width), lambda i: (0, 0)),
        ],
        out_specs=[block, whole, whole],
        out_shape=[
            jax.ShapeDtypeStruct((tokens, width), jnp.bfloat16),
            jax.ShapeDtypeStruct((memory_rows, width), jnp.bfloat16),
            jax.ShapeDtypeStruct((memory_rows, width), jnp.bfloat16),
        ],
        scratch_shapes=[
            pltpu.VMEM((width, memory_rows), jnp.bfloat16),
            pltpu.VMEM((memory_rows, width), jnp.float32),
            pltpu.VMEM((memory_rows, width), jnp.float32),
        ],
        compiler_params=pltpu.CompilerParams(vmem_limit_bytes=24 * 1024 * 1024),
        name="attend_grads",
    )(query, key, value, prob, hidden_out, coefficient, score_out)


def head_kernel(
    counts_ref,
    sums_ref,
    hidden_ref,
    weighted_ref,
    rank_ref,
    visits_ref,
    hidden_grad_ref,
    coefficient_ref,
    log_ref,
    loss_ref,
):
    tokens, slots = sums_ref.shape[1], rank_ref.shape[1]
    per_tactic = tokens // slots
    model_width = 4 * hidden_ref.shape[1]
    sums = jnp.concatenate([sums_ref[...], jnp.zeros((6, tokens), jnp.float32)], axis=0).T
    inverse = lax.rsqrt(sums[:, 0:1] / model_width + 1e-06)
    raw = sums[:, 1:2]
    token = lax.broadcasted_iota(jnp.int32, (tokens, slots), 0)
    first = lax.broadcasted_iota(jnp.int32, (tokens, slots), 1) * per_tactic
    member = (token >= first) & (token < first + per_tactic)
    logits = jnp.sum(jnp.where(member, inverse * raw, 0.0), axis=0, keepdims=True) / per_tactic
    live = rank_ref[...] < counts_ref[0]
    masked = jnp.where(live, logits, -1e30)
    top_value = jnp.max(masked, axis=1, keepdims=True)
    exponent = jnp.where(live, jnp.exp(masked - top_value), 0.0)
    log_total = top_value + jnp.log(jnp.sum(exponent, axis=1, keepdims=True))
    log_weight = jnp.where(live, logits - log_total, 0.0)
    visit_mass = jnp.where(live, visits_ref[...].astype(jnp.float32), 0.0)
    target = visit_mass / jnp.sum(visit_mass, axis=1, keepdims=True)
    log_ref[...] = log_weight
    loss_ref[...] = -jnp.sum(target * log_weight, axis=1, keepdims=True)
    logit_grad = jnp.where(live, jnp.exp(log_weight) - target, 0.0) / per_tactic
    tok_grad = jnp.sum(jnp.where(member, logit_grad, 0.0), axis=1, keepdims=True)
    near = inverse * tok_grad
    far = inverse * inverse * inverse * tok_grad * raw / model_width
    hidden_grad_ref[...] = (near * weighted_ref[...] - hidden_ref[...] * far).astype(jnp.bfloat16)
    coefficient_ref[:, 0:1] = near
    coefficient_ref[:, 1:2] = far


def policy_head(counts, sums, hidden, weighted, rank, visits):
    in_vmem = pl.BlockSpec(memory_space=pltpu.VMEM)
    tokens, width = hidden.shape
    slots = rank.shape[1]
    return pl.pallas_call(
        head_kernel,
        in_specs=[pl.BlockSpec(memory_space=pltpu.SMEM)] + [in_vmem] * 5,
        out_specs=[in_vmem] * 4,
        out_shape=[
            jax.ShapeDtypeStruct((tokens, width), jnp.bfloat16),
            jax.ShapeDtypeStruct((tokens, 2), jnp.float32),
            jax.ShapeDtypeStruct((1, slots), jnp.float32),
            jax.ShapeDtypeStruct((1, 1), jnp.float32),
        ],
        compiler_params=pltpu.CompilerParams(vmem_limit_bytes=16 * 1024 * 1024),
        name="policy_head",
    )(counts, sums, hidden, weighted, rank, visits)


def matmul(left, right, contract=(((1,), (0,)), ((), ()))):
    return lax.dot_general(left, right, contract, preferred_element_type=jnp.float32)


def body(dec_states, memory, counts, rank, visits, w_query, w_key, w_value, w_out, gain, w_score):
    model_width, width = w_query.shape
    slot_here, per_tactic = dec_states.shape[1:3]
    own_rows = slot_here * per_tactic
    slots = 16 * slot_here
    total_rows = slots * per_tactic
    slice_width = model_width // 4
    cand = lax.axis_index("cand")
    goal = lax.axis_index("goal")
    y = cand & 3
    core = goal & 1
    goal_bits = pair_bits(goal >> 1)

    own = jnp.concatenate([dec_states[0].reshape(own_rows, model_width), memory[0]], axis=0)
    bits = pair_bits(cand >> 2) + pair_bits(y)
    parts, cut = gather_cand(own, bits, cut_out_weights(w_out, y, core))
    rows = jnp.concatenate(
        [part[..., :own_rows, :].reshape(total_rows, -1) for part in parts], axis=1
    )
    memory_all = jnp.concatenate(
        [part[..., own_rows:, :].reshape(16 * memory.shape[1], -1) for part in parts], axis=1
    )
    fetched = fetch_out_weights(cut)

    query = low(matmul(rows, w_query))
    key = low(matmul(memory_all, w_key))
    value = low(matmul(memory_all, w_value))
    mixed, prob = attend(query, key, value)

    weighted = gain * w_score
    score_out = jnp.sum(w_out.astype(jnp.float32) * weighted[None, :], axis=1)
    order = jnp.array([c * slot_here + s for c in cand_order() for s in range(slot_here)], jnp.int32)
    pick = order[None, :] == jnp.arange(slots, dtype=jnp.int32)[:, None]
    rank_here = jnp.sum(jnp.where(pick, rank[0][:, None], 0), axis=0, keepdims=True)
    visits_here = jnp.sum(jnp.where(pick, visits[0][:, None], 0), axis=0, keepdims=True)

    mixed_line, (got, other) = gather_heads(mixed, fetched)
    w_slice = join_out_weights(w_out, got, other, y, core)
    attended = sum_line(matmul(mixed_line, w_slice))
    hidden = lax.dynamic_slice_in_dim(rows, y * slice_width, slice_width, 1).astype(jnp.float32)
    hidden = hidden + attended
    weighted_slice = lax.dynamic_slice_in_dim(weighted, y * slice_width, slice_width, 0)
    sums = jnp.stack([jnp.sum(hidden * hidden, axis=1), jnp.sum(hidden * weighted_slice, axis=1)])
    kept, sums = scatter_heads_start(low(matmul(low(hidden), w_slice, SUM_COLUMNS)), sums, width)
    hidden_out = scatter_heads_end(kept, width)
    hidden_grad, coefficient, log_weight, loss = policy_head(
        counts, sums, hidden, weighted_slice[None, :], rank_here, visits_here
    )

    keep, send = core_halves(hidden_grad, core)
    taken = swap_goal(send, 1)
    mixed_other = swap_goal(mixed_line, 1)
    quarter = slice_width // 4
    out_lines = jnp.stack(
        [
            low(
                matmul(mixed_line, keep[:, i * quarter : (i + 1) * quarter], SUM_ROWS)
                + matmul(mixed_other, taken[:, i * quarter : (i + 1) * quarter], SUM_ROWS)
            )
            for i in (0, 1)
        ]
    )
    out_lines = out_lines.reshape(2, 4, width, quarter).transpose(1, 0, 2, 3)
    hidden_out, out_lines = lax.optimization_barrier((hidden_out, out_lines))
    pairs = []
    for g in range(8):
        for c in range(16):
            goal_to = 2 * (c & 3) + (g & 1)
            pairs.append((16 * g + c, 16 * goal_to + (c ^ (g >> 1))))

    query_grad, key_grad, value_grad = attend_grads(
        query, key, value, prob, hidden_out, coefficient, score_out[None, :]
    )
    rows_both = share_columns(rows, core)
    memory_both = share_columns(memory_all, core)
    value_lines = both_terms(memory_both, value_grad)
    first_lines = jnp.stack([value_lines.reshape(4, -1, width), out_lines.reshape(4, -1, width)])
    grad_value, grad_out = sum_z(first_lines, goal_bits)
    grad_out = jnp.concatenate([grad_out[:width], grad_out[width:]], axis=1)
    grad_out = lax.ppermute(grad_out, ("goal", "cand"), pairs)
    key_lines = both_terms(memory_both, key_grad)
    query_lines = both_terms(rows_both, query_grad)
    both_lines = jnp.concatenate([query_lines, key_lines]).reshape(2, 4, -1, width)
    grad_both = sum_z(both_lines, goal_bits)
    own_slots = cand * slot_here + jnp.arange(slot_here, dtype=jnp.int32)
    own_log = jnp.sum(
        jnp.where(own_slots[:, None] == order[None, :], log_weight, 0.0), axis=1
    )
    return own_log[None, :], loss[0], grad_both[0], grad_both[1], grad_value, grad_out


def solution(mesh):
    return jax.shard_map(
        body,
        mesh=mesh,
        in_specs=(
            P("goal", "cand", None, None),
            P("goal", "cand", None),
            P("goal"),
            P("goal", None),
            P("goal", None),
            P(None, "cand"),
            P(None, "cand"),
            P(None, "cand"),
            P("cand", None),
            P(),
            P(),
        ),
        out_specs=(
            P("goal", "cand"),
            P("goal"),
            P("goal", "cand"),
            P("goal", "cand"),
            P("goal", "cand"),
            P("cand", "goal"),
        ),
        check_vma=False,
    )
```

```python
import jax
import jax.numpy as jnp
from jax import lax
from jax.experimental import pallas as pl
from jax.experimental.pallas import tpu as pltpu
from jax.sharding import PartitionSpec as P

HD = 64
HEADS_HERE = 4
TOKEN_BLOCK = 256
X_MASKS = (4, 12)
Y_MASKS = (1, 3)
CAND_MASKS = X_MASKS + Y_MASKS
GOAL_MASKS = (2, 6)
PART_ORDERS = ((0, 1, 2, 3), (1, 0, 3, 2), (2, 3, 0, 1), (3, 2, 1, 0))
SUM_ROWS = (((0,), (0,)), ((), ()))
SUM_COLUMNS = (((1,), (1,)), ((), ()))


def swap_cand(values, mask):
    return lax.ppermute(values, "cand", [(i, i ^ mask) for i in range(16)])


def swap_goal(values, mask):
    return lax.ppermute(values, "goal", [(i, i ^ mask) for i in range(8)])


def exchange(parts, masks, swap=swap_cand):
    parts = lax.optimization_barrier(list(parts))
    return lax.optimization_barrier([swap(part, mask) for part, mask in zip(parts, masks)])


def plus(left, right):
    return left.astype(jnp.float32) + right.astype(jnp.float32)


def low(values):
    return values.astype(jnp.bfloat16)


def pair_bits(coordinate):
    high = coordinate >> 1
    return ((coordinate & 1) ^ high, high)


def cand_order():
    order = []
    for position in range(16):
        bits = [(position >> i) & 1 for i in range(4)]
        order.append(4 * (bits[0] ^ (3 * bits[1])) + (bits[2] ^ (3 * bits[3])))
    return order


def gather_cand(own, bits, early):
    parts = [part[None, None, None, None] for part in jnp.split(own, 4, axis=1)]
    for step in range(4):
        masks = [CAND_MASKS[order[step]] for order in PART_ORDERS]
        if step < 2:
            others = exchange(parts, masks)
        else:
            if step == 3:
                parts, early = lax.optimization_barrier((parts, early))
            others = [swap_cand(part, mask) for part, mask in zip(parts, masks)]
            if step == 3:
                others, early = lax.optimization_barrier((others, early))
        merged = []
        for part, other, order in zip(parts, others, PART_ORDERS):
            bit = bits[order[step]]
            first = jnp.where(bit == 0, part, other)
            second = jnp.where(bit == 0, other, part)
            merged.append(jnp.concatenate([first, second], axis=3 - order[step]))
        parts = merged
    return parts, early


def cut_out_weights(w_out, y, core):
    height, width = w_out.shape[0] // 2, w_out.shape[1] // 4
    return [
        lax.dynamic_slice(w_out, (core * height, (y ^ mask) * width), (height, width))
        for mask in (1, 3, 2)
    ]


def fetch_out_weights(cut):
    got = jnp.concatenate(exchange(cut, (1, 3, 2)), axis=0)
    return got, swap_goal(got, 1)


def join_out_weights(w_out, got, other, y, core):
    height, width = got.shape[0] // 3, got.shape[1]
    first = jnp.where(core == 0, got, other).reshape(3, height, width)
    second = jnp.where(core == 0, other, got).reshape(3, height, width)
    received = jnp.stack([first, second], axis=1).reshape(6 * height, width)
    own = lax.dynamic_slice_in_dim(w_out, y * width, width, 1)
    return jnp.concatenate([own, received], axis=0)


def gather_heads(mixed, fetched):
    halves = jnp.split(mixed, 2, axis=0)
    near = exchange(halves, Y_MASKS)
    pairs = [jnp.concatenate([half, other], axis=1) for half, other in zip(halves, near)]
    pairs, fetched = lax.optimization_barrier((pairs, fetched))
    far = exchange(pairs, Y_MASKS[::-1])
    width = mixed.shape[1]
    second = jnp.concatenate(
        [halves[1], far[1][:, :width], near[1], far[1][:, width:]], axis=1
    )
    first = jnp.concatenate([halves[0], near[0], far[0]], axis=1)
    return jnp.concatenate([first, second], axis=0), fetched


def sum_line(values):
    parts = jnp.split(low(values), 2, axis=1)
    for masks in (X_MASKS, X_MASKS[::-1]):
        others = exchange(parts, masks)
        totals = [plus(part, other) for part, other in zip(parts, others)]
        parts = [low(total) for total in totals]
    return jnp.concatenate(totals, axis=1)


def scatter_heads_start(values, sums, width):
    halves = jnp.split(values, 2, axis=0)
    blocks = [[half[:, i * width : (i + 1) * width] for i in range(4)] for half in halves]
    keep = [jnp.concatenate(blocks[0][:2], axis=1), jnp.concatenate(blocks[1][::2], axis=1)]
    send = [jnp.concatenate(blocks[0][2:], axis=1), jnp.concatenate(blocks[1][1::2], axis=1)]
    others = exchange(send + [sums] * 3, Y_MASKS[::-1] + (1, 3, 2))
    kept = [low(plus(part, other)) for part, other in zip(keep, others)]
    return kept, (sums + others[2]) + (others[3] + others[4])


def scatter_heads_end(kept, width):
    others = exchange([part[:, width:] for part in kept], Y_MASKS)
    return jnp.concatenate(
        [plus(part[:, :width], other) for part, other in zip(kept, others)], axis=0
    )


def core_halves(values, core):
    half = values.shape[1] // 2
    left, right = values[:, :half], values[:, half:]
    return jnp.where(core == 0, left, right), jnp.where(core == 0, right, left)


def share_columns(values, core):
    quarters = [core_halves(part, core) for part in jnp.split(values, 4, axis=1)]
    quarters = [quarters[i] for i in (0, 1, 3, 2)]
    keep = jnp.concatenate([quarter[0] for quarter in quarters], axis=1)
    send = jnp.concatenate([quarter[1] for quarter in quarters], axis=1)
    return keep, swap_goal(send, 1)


def both_terms(values, grads):
    return low(
        matmul(values[0], grads, SUM_ROWS) + matmul(values[1], swap_goal(grads, 1), SUM_ROWS)
    )


def sum_z_step(zeros, ones, bits, turn):
    which = (turn, 1 - turn)
    sends = [jnp.where(bits[w] == 0, one, zero) for w, zero, one in zip(which, zeros, ones)]
    keeps = [jnp.where(bits[w] == 0, zero, one) for w, zero, one in zip(which, zeros, ones)]
    others = exchange(sends, [GOAL_MASKS[w] for w in which], swap_goal)
    return [low(plus(part, other)) for part, other in zip(keeps, others)]


def sum_z_start(lines, bits):
    count, _, height, width = lines.shape
    lines = lines.reshape(count, 2, 2, height, width)
    parts = [lines[:, :, :, : height // 2], lines[:, :, :, height // 2 :]]
    zeros = [parts[0][:, :, 0], parts[1][:, 0]]
    ones = [parts[0][:, :, 1], parts[1][:, 1]]
    return sum_z_step(zeros, ones, bits, 0)


def sum_z_end(sums, bits):
    sums = sum_z_step([part[:, 0] for part in sums], [part[:, 1] for part in sums], bits, 1)
    return jnp.concatenate(sums, axis=1)


def sum_z(lines, bits):
    return sum_z_end(sum_z_start(lines, bits), bits)


def head_mask(head, dtype):
    lane = lax.broadcasted_iota(jnp.int32, (1, HEADS_HERE * HD), 1)
    inside = (lane >= head * HD) & (lane < (head + 1) * HD)
    return jnp.where(inside, 1.0, 0.0).astype(dtype)


def attend_kernel(query_ref, key_ref, value_ref, mixed_ref, prob_ref, flipped_ref):
    @pl.when(pl.program_id(0) == 0)
    def _():
        flipped_ref[...] = value_ref[...].astype(jnp.float32).T.astype(jnp.bfloat16)

    query = query_ref[...] * jnp.bfloat16(HD ** (-0.5))
    key = key_ref[...]
    outs = []
    for head in range(HEADS_HERE):
        scores = matmul(key * head_mask(head, jnp.bfloat16), query, SUM_COLUMNS)
        exponent = jnp.exp(scores - jnp.max(scores, axis=0, keepdims=True))
        share = 1.0 / jnp.sum(exponent, axis=0, keepdims=True)
        prob = (exponent * share).astype(jnp.bfloat16)
        prob_ref[head] = prob
        outs.append(matmul(flipped_ref[head * HD : (head + 1) * HD, :], prob))
    mixed_ref[...] = jnp.concatenate(outs, axis=0).T.astype(jnp.bfloat16)


def attend(query, key, value):
    tokens, width = query.shape
    memory_rows = key.shape[0]
    whole = pl.BlockSpec((memory_rows, width), lambda i: (0, 0))
    block = pl.BlockSpec((TOKEN_BLOCK, width), lambda i: (i, 0))
    return pl.pallas_call(
        attend_kernel,
        grid=(tokens // TOKEN_BLOCK,),
        in_specs=[block, whole, whole],
        out_specs=[
            block,
            pl.BlockSpec((HEADS_HERE, memory_rows, TOKEN_BLOCK), lambda i: (0, 0, i)),
        ],
        out_shape=[
            jax.ShapeDtypeStruct((tokens, width), jnp.bfloat16),
            jax.ShapeDtypeStruct((HEADS_HERE, memory_rows, tokens), jnp.bfloat16),
        ],
        scratch_shapes=[pltpu.VMEM((width, memory_rows), jnp.bfloat16)],
        compiler_params=pltpu.CompilerParams(vmem_limit_bytes=24 * 1024 * 1024),
        name="attend",
    )(query, key, value)


def attend_grads_kernel(
    query_ref,
    key_ref,
    value_ref,
    prob_ref,
    hidden_out_ref,
    coefficient_ref,
    score_out_ref,
    query_grad_ref,
    key_grad_ref,
    value_grad_ref,
    flipped_ref,
    key_sum_ref,
    value_sum_ref,
):
    step = pl.program_id(0)

    @pl.when(step == 0)
    def _():
        flipped_ref[...] = key_ref[...].astype(jnp.float32).T.astype(jnp.bfloat16)
        key_sum_ref[...] = jnp.zeros_like(key_sum_ref)
        value_sum_ref[...] = jnp.zeros_like(value_sum_ref)

    coefficient = coefficient_ref[...]
    mixed_grad = coefficient[:, 0:1] * score_out_ref[...] - coefficient[:, 1:2] * hidden_out_ref[...]
    mixed_grad = mixed_grad.astype(jnp.bfloat16)
    query = query_ref[...]
    value = value_ref[...]
    outs = []
    key_sum = key_sum_ref[...]
    value_sum = value_sum_ref[...]
    for head in range(HEADS_HERE):
        prob_grad = matmul(value * head_mask(head, jnp.bfloat16), mixed_grad, SUM_COLUMNS)
        prob_low = prob_ref[head]
        prob = prob_low.astype(jnp.float32)
        delta = jnp.sum(prob * prob_grad, axis=0, keepdims=True)
        score_grad = (prob * ((prob_grad - delta) * HD ** (-0.5))).astype(jnp.bfloat16)
        mask = head_mask(head, jnp.float32)
        key_sum = key_sum + matmul(score_grad, query) * mask
        value_sum = value_sum + matmul(prob_low, mixed_grad) * mask
        outs.append(matmul(flipped_ref[head * HD : (head + 1) * HD, :], score_grad))
    key_sum_ref[...] = key_sum
    value_sum_ref[...] = value_sum
    query_grad_ref[...] = jnp.concatenate(outs, axis=0).T.astype(jnp.bfloat16)

    @pl.when(step == pl.num_programs(0) - 1)
    def _():
        key_grad_ref[...] = key_sum_ref[...].astype(jnp.bfloat16)
        value_grad_ref[...] = value_sum_ref[...].astype(jnp.bfloat16)


def attend_grads(query, key, value, prob, hidden_out, coefficient, score_out):
    tokens, width = query.shape
    memory_rows = key.shape[0]
    whole = pl.BlockSpec((memory_rows, width), lambda i: (0, 0))
    block = pl.BlockSpec((TOKEN_BLOCK, width), lambda i: (i, 0))
    return pl.pallas_call(
        attend_grads_kernel,
        grid=(tokens // TOKEN_BLOCK,),
        in_specs=[
            block,
            whole,
            whole,
            pl.BlockSpec((HEADS_HERE, memory_rows, TOKEN_BLOCK), lambda i: (0, 0, i)),
            block,
            pl.BlockSpec((TOKEN_BLOCK, 2), lambda i: (i, 0)),
            pl.BlockSpec((1, width), lambda i: (0, 0)),
        ],
        out_specs=[block, whole, whole],
        out_shape=[
            jax.ShapeDtypeStruct((tokens, width), jnp.bfloat16),
            jax.ShapeDtypeStruct((memory_rows, width), jnp.bfloat16),
            jax.ShapeDtypeStruct((memory_rows, width), jnp.bfloat16),
        ],
        scratch_shapes=[
            pltpu.VMEM((width, memory_rows), jnp.bfloat16),
            pltpu.VMEM((memory_rows, width), jnp.float32),
            pltpu.VMEM((memory_rows, width), jnp.float32),
        ],
        compiler_params=pltpu.CompilerParams(vmem_limit_bytes=24 * 1024 * 1024),
        name="attend_grads",
    )(query, key, value, prob, hidden_out, coefficient, score_out)


def head_kernel(
    counts_ref,
    sums_ref,
    hidden_ref,
    weighted_ref,
    rank_ref,
    visits_ref,
    hidden_grad_ref,
    coefficient_ref,
    log_ref,
    loss_ref,
):
    tokens, slots = sums_ref.shape[1], rank_ref.shape[1]
    per_tactic = tokens // slots
    model_width = 4 * hidden_ref.shape[1]
    sums = jnp.concatenate([sums_ref[...], jnp.zeros((6, tokens), jnp.float32)], axis=0).T
    inverse = lax.rsqrt(sums[:, 0:1] / model_width + 1e-06)
    raw = sums[:, 1:2]
    token = lax.broadcasted_iota(jnp.int32, (tokens, slots), 0)
    first = lax.broadcasted_iota(jnp.int32, (tokens, slots), 1) * per_tactic
    member = (token >= first) & (token < first + per_tactic)
    logits = jnp.sum(jnp.where(member, inverse * raw, 0.0), axis=0, keepdims=True) / per_tactic
    live = rank_ref[...] < counts_ref[0]
    masked = jnp.where(live, logits, -1e30)
    top_value = jnp.max(masked, axis=1, keepdims=True)
    exponent = jnp.where(live, jnp.exp(masked - top_value), 0.0)
    log_total = top_value + jnp.log(jnp.sum(exponent, axis=1, keepdims=True))
    log_weight = jnp.where(live, logits - log_total, 0.0)
    visit_mass = jnp.where(live, visits_ref[...].astype(jnp.float32), 0.0)
    target = visit_mass / jnp.sum(visit_mass, axis=1, keepdims=True)
    log_ref[...] = log_weight
    loss_ref[...] = -jnp.sum(target * log_weight, axis=1, keepdims=True)
    logit_grad = jnp.where(live, jnp.exp(log_weight) - target, 0.0) / per_tactic
    tok_grad = jnp.sum(jnp.where(member, logit_grad, 0.0), axis=1, keepdims=True)
    near = inverse * tok_grad
    far = inverse * inverse * inverse * tok_grad * raw / model_width
    hidden_grad_ref[...] = (near * weighted_ref[...] - hidden_ref[...] * far).astype(jnp.bfloat16)
    coefficient_ref[:, 0:1] = near
    coefficient_ref[:, 1:2] = far


def policy_head(counts, sums, hidden, weighted, rank, visits):
    in_vmem = pl.BlockSpec(memory_space=pltpu.VMEM)
    tokens, width = hidden.shape
    slots = rank.shape[1]
    return pl.pallas_call(
        head_kernel,
        in_specs=[pl.BlockSpec(memory_space=pltpu.SMEM)] + [in_vmem] * 5,
        out_specs=[in_vmem] * 4,
        out_shape=[
            jax.ShapeDtypeStruct((tokens, width), jnp.bfloat16),
            jax.ShapeDtypeStruct((tokens, 2), jnp.float32),
            jax.ShapeDtypeStruct((1, slots), jnp.float32),
            jax.ShapeDtypeStruct((1, 1), jnp.float32),
        ],
        compiler_params=pltpu.CompilerParams(vmem_limit_bytes=16 * 1024 * 1024),
        name="policy_head",
    )(counts, sums, hidden, weighted, rank, visits)


def matmul(left, right, contract=(((1,), (0,)), ((), ()))):
    return lax.dot_general(left, right, contract, preferred_element_type=jnp.float32)


def body(dec_states, memory, counts, rank, visits, w_query, w_key, w_value, w_out, gain, w_score):
    model_width, width = w_query.shape
    slot_here, per_tactic = dec_states.shape[1:3]
    own_rows = slot_here * per_tactic
    slots = 16 * slot_here
    total_rows = slots * per_tactic
    slice_width = model_width // 4
    cand = lax.axis_index("cand")
    goal = lax.axis_index("goal")
    y = cand & 3
    core = goal & 1
    goal_bits = pair_bits(goal >> 1)

    own = jnp.concatenate([dec_states[0].reshape(own_rows, model_width), memory[0]], axis=0)
    bits = pair_bits(cand >> 2) + pair_bits(y)
    parts, cut = gather_cand(own, bits, cut_out_weights(w_out, y, core))
    rows = jnp.concatenate(
        [part[..., :own_rows, :].reshape(total_rows, -1) for part in parts], axis=1
    )
    memory_all = jnp.concatenate(
        [part[..., own_rows:, :].reshape(16 * memory.shape[1], -1) for part in parts], axis=1
    )
    fetched = fetch_out_weights(cut)

    query = low(matmul(rows, w_query))
    key = low(matmul(memory_all, w_key))
    value = low(matmul(memory_all, w_value))
    mixed, prob = attend(query, key, value)

    weighted = gain * w_score
    score_out = jnp.sum(w_out.astype(jnp.float32) * weighted[None, :], axis=1)
    order = jnp.array([c * slot_here + s for c in cand_order() for s in range(slot_here)], jnp.int32)
    pick = order[None, :] == jnp.arange(slots, dtype=jnp.int32)[:, None]
    rank_here = jnp.sum(jnp.where(pick, rank[0][:, None], 0), axis=0, keepdims=True)
    visits_here = jnp.sum(jnp.where(pick, visits[0][:, None], 0), axis=0, keepdims=True)

    mixed_line, (got, other) = gather_heads(mixed, fetched)
    w_slice = join_out_weights(w_out, got, other, y, core)
    attended = sum_line(matmul(mixed_line, w_slice))
    hidden = lax.dynamic_slice_in_dim(rows, y * slice_width, slice_width, 1).astype(jnp.float32)
    hidden = hidden + attended
    weighted_slice = lax.dynamic_slice_in_dim(weighted, y * slice_width, slice_width, 0)
    sums = jnp.stack([jnp.sum(hidden * hidden, axis=1), jnp.sum(hidden * weighted_slice, axis=1)])
    kept, sums = scatter_heads_start(low(matmul(low(hidden), w_slice, SUM_COLUMNS)), sums, width)
    hidden_out = scatter_heads_end(kept, width)
    hidden_grad, coefficient, log_weight, loss = policy_head(
        counts, sums, hidden, weighted_slice[None, :], rank_here, visits_here
    )

    keep, send = core_halves(hidden_grad, core)
    taken = swap_goal(send, 1)
    mixed_other = swap_goal(mixed_line, 1)
    quarter = slice_width // 4
    out_lines = jnp.stack(
        [
            low(
                matmul(mixed_line, keep[:, i * quarter : (i + 1) * quarter], SUM_ROWS)
                + matmul(mixed_other, taken[:, i * quarter : (i + 1) * quarter], SUM_ROWS)
            )
            for i in (0, 1)
        ]
    )
    out_lines = out_lines.reshape(2, 4, width, quarter).transpose(1, 0, 2, 3)
    pairs = []
    for g in range(8):
        for c in range(16):
            goal_to = 2 * (c & 3) + (g & 1)
            pairs.append((16 * g + c, 16 * goal_to + (c ^ (g >> 1))))

    query_grad, key_grad, value_grad = attend_grads(
        query, key, value, prob, hidden_out, coefficient, score_out[None, :]
    )
    rows_both = share_columns(rows, core)
    memory_both = share_columns(memory_all, core)
    value_lines = both_terms(memory_both, value_grad)
    first_lines = jnp.stack([value_lines.reshape(4, -1, width), out_lines.reshape(4, -1, width)])
    grad_value, grad_out = sum_z(first_lines, goal_bits)
    grad_out = jnp.concatenate([grad_out[:width], grad_out[width:]], axis=1)
    grad_out = lax.ppermute(grad_out, ("goal", "cand"), pairs)
    key_lines = both_terms(memory_both, key_grad)
    query_lines = both_terms(rows_both, query_grad)
    both_lines = jnp.concatenate([query_lines, key_lines]).reshape(2, 4, -1, width)
    grad_both = sum_z(both_lines, goal_bits)
    own_slots = cand * slot_here + jnp.arange(slot_here, dtype=jnp.int32)
    own_log = jnp.sum(
        jnp.where(own_slots[:, None] == order[None, :], log_weight, 0.0), axis=1
    )
    return own_log[None, :], loss[0], grad_both[0], grad_both[1], grad_value, grad_out


def solution(mesh):
    return jax.shard_map(
        body,
        mesh=mesh,
        in_specs=(
            P("goal", "cand", None, None),
            P("goal", "cand", None),
            P("goal"),
            P("goal", None),
            P("goal", None),
            P(None, "cand"),
            P(None, "cand"),
            P(None, "cand"),
            P("cand", None),
            P(),
            P(),
        ),
        out_specs=(
            P("goal", "cand"),
            P("goal"),
            P("goal", "cand"),
            P("goal", "cand"),
            P("goal", "cand"),
            P("cand", "goal"),
        ),
        check_vma=False,
    )
```
